32 devices in a mesh: groups: 2 (over x), seq: 8 (over z, y), slab: 2 (over core).
Axes of the slice: x: 2, y: 2, z: 4, core: 2. Of those that a mesh axis runs over, the one named last changes fastest.
Arguments:
- noise: float32 [128, 64], P(('groups', 'seq')), parts along dimension 0, may hold values from -6 to 6
- timesteps: int32 [4, 4], P('groups'), parts along dimension 0, may hold values from 0 to 999, as said below
- fine_counts: int32 [4], P('groups'), parts along dimension 0, may hold values from 1 to 3
- w_in: bfloat16 [64, 2560], replicated, may hold values from -0.75 to 0.75
- w_query: bfloat16 [2560, 1024], P(None, 'seq'), may hold values from -24 to 24
- w_key: bfloat16 [2560, 1024], P(None, 'seq'), may hold values from -0.125 to 0.125
- w_value: bfloat16 [2560, 1024], P(None, 'seq'), may hold values from -0.125 to 0.125
- w_out: bfloat16 [1024, 2560], P('seq'), may hold values from -0.1875 to 0.1875
- w_final: float32 [2560, 64], replicated, may hold values from -0.125 to 0.125
- mod_scale: float32 [2560], replicated, may hold values from -0.9 to 0.9
- mod_shift: float32 [2560], replicated, may hold values from -3 to 3
- skip_gain: float32 [2560], replicated, may hold values from 0.3 to 1.2
Outputs:
- slab_ends: float32 [2, 128, 64], P('slab', ('groups', 'seq')), parts along dimension 1
The draws below stay inside these ranges and needn't reach their ends.
There are 2 independent parts, one for each index of `groups`. The reference program is written for one: setup_inputs(seed, part) draws one part's arguments, and reference() takes and returns one part's arrays. A program takes and returns all parts, laid end to end along the dimension named above; an argument that names none is the same for every part. Nothing has to cross between parts.
Inputs may be any that keep to these rules, and one draw needn't show every extreme that they name: `timesteps`: within a slab the points up to column fine_counts strictly fall; the last used point of a slab is the first point of the next; some slab takes exactly 3 steps.
All inputs are finite; a program needn't handle non-finite values.
Results may differ from the reference program's by a relative error of at most 0.013.
Values may be sent and summed in bfloat16 or wider, within the bound.
No kernel may reach another device: no remote copies, remote signals or barrier semaphores. Data moves between devices by JAX's collectives and lax.ppermute only.
A program may use at most 64 MiB of HBM per device.

```python
import math
import jax
import jax.numpy as jnp
from jax import lax

C = 64
D = 2560
HEAD_SIZE = 128
HEADS = 8
TOKENS = 64
FINE_MAX = 3
ITERS = 1
N_SLAB = 2


def plan_draw(seed_key, part):
    base_key = jax.random.fold_in(seed_key, 7)
    split_keys = jax.random.split(base_key, 7)
    slab_ids = jnp.arange(N_SLAB, dtype=jnp.int32)
    offset = jax.random.randint(split_keys[0], (), 0, 4, dtype=jnp.int32)
    code = (jnp.asarray(part).astype(jnp.int32) + offset) % 4
    forced_slab = code // 2 % N_SLAB
    counts_other = 1 + (code + slab_ids) % (FINE_MAX - 1)
    step_counts = jnp.where(slab_ids == forced_slab, FINE_MAX, counts_other).astype(jnp.int32)
    first_time = 999 - jax.random.randint(split_keys[2], (), 0, 20, dtype=jnp.int32)
    last_time = jax.random.randint(split_keys[3], (), 0, 20, dtype=jnp.int32)
    gap_weights = jax.random.randint(split_keys[4], (N_SLAB,), 2, 5, dtype=jnp.int32)
    gap_cumul = jnp.concatenate([jnp.zeros((1,), jnp.int32), jnp.cumsum(gap_weights).astype(jnp.int32)])
    bounds = first_time - (first_time - last_time) * gap_cumul // gap_cumul[-1]
    increments = jax.random.randint(split_keys[5], (N_SLAB, FINE_MAX), 1, 4, dtype=jnp.int32)
    inc_cumul = jnp.concatenate([jnp.zeros((N_SLAB, 1), jnp.int32), jnp.cumsum(increments, axis=1).astype(jnp.int32)], axis=1)
    position = jnp.arange(FINE_MAX + 1, dtype=jnp.int32)[None, :]
    live_total = jnp.sum(jnp.where(position == step_counts[:, None], inc_cumul, 0), axis=1)
    upper = bounds[:-1][:, None]
    lower = bounds[1:][:, None]
    inside = upper - (upper - lower) * inc_cumul // live_total[:, None]
    filler = jax.random.randint(split_keys[6], (N_SLAB, FINE_MAX + 1), 0, 1000, dtype=jnp.int32)
    plan = jnp.where(position <= step_counts[:, None], inside, filler).astype(jnp.int32)
    return (step_counts, plan)


def draw_fine_counts(key, part):
    return plan_draw(key, part)[0]


def draw_timesteps(key, part):
    return plan_draw(key, part)[1]


def draw_w_query(key, part):
    base_key = jax.random.fold_in(key, 11)
    first_key = jax.random.fold_in(base_key, 0)
    entries = jax.random.normal(first_key, (D, HEADS * HEAD_SIZE), jnp.float32) * D ** (-0.5)
    return jnp.clip(entries, -24.0, 24.0).astype(jnp.bfloat16)


def block_scale(key, shape, pieces, low, largest):
    factor_of, own = 1.0, jax.random.fold_in(key, 6)
    for dim, parts in pieces:
        steps = jnp.exp(jax.random.uniform(jax.random.fold_in(own, dim), (parts,), jnp.float32, low / len(pieces), largest / len(pieces)))
        factor_of = factor_of * jnp.repeat(steps, shape[dim] // parts).reshape([-1 if axis == dim else 1 for axis in range(len(shape))])
    return factor_of


def gaussian(own_key, dims, scale, bound, cuts=(), held_as=jnp.bfloat16):
    array = jax.random.normal(own_key, dims, jnp.float32) * scale
    if len(cuts) > 0:
        array = block_scale(own_key, dims, cuts, -0.22, 0.18) * array
    return jnp.clip(array, min=-bound, max=bound).astype(held_as)


def setup_inputs(seed: int = 0, part: int = 0) -> dict:
    arg_keys = jax.random.split(jax.random.key(seed), 13)
    part_keys = jax.random.split(jax.random.fold_in(arg_keys[12], part), 13)
    noise = gaussian(part_keys[0], (TOKENS, C), 1.0, 6.0, ((0, 8),), jnp.float32)
    timesteps = draw_timesteps(jax.random.fold_in(jax.random.fold_in(arg_keys[12], part), 71), part)
    fine_counts = draw_fine_counts(jax.random.fold_in(jax.random.fold_in(arg_keys[12], part), 71), part)
    w_in = gaussian(arg_keys[3], (C, D), C ** -0.5, 0.75)
    w_query = draw_w_query(jax.random.fold_in(arg_keys[12], 71), part)
    w_key = gaussian(arg_keys[5], (D, HEADS * HEAD_SIZE), D ** -0.5, 0.125, ((1, 8),))
    w_value = gaussian(arg_keys[6], (D, HEADS * HEAD_SIZE), D ** -0.5, 0.125, ((1, 8),))
    w_out = gaussian(arg_keys[7], (HEADS * HEAD_SIZE, D), (HEADS * HEAD_SIZE) ** -0.5, 0.1875, ((0, 8),))
    w_final = gaussian(arg_keys[8], (D, C), D ** -0.5, 0.125, (), jnp.float32)
    mod_scale = jnp.clip(jax.random.uniform(arg_keys[9], (D,), jnp.float32, -0.9, 0.9), -0.9, 0.9)
    mod_shift = gaussian(arg_keys[10], (D,), 0.6, 3.0, (), jnp.float32)
    skip_gain = jnp.clip(jax.random.uniform(arg_keys[11], (D,), jnp.float32, 0.3, 1.2), 0.3, 1.2)
    return {"noise": noise, "timesteps": timesteps, "fine_counts": fine_counts, "w_in": w_in, "w_query": w_query, "w_key": w_key, "w_value": w_value, "w_out": w_out, "w_final": w_final, "mod_scale": mod_scale, "mod_shift": mod_shift, "skip_gain": skip_gain}


def attend(queries, key_rows, value_rows, head_size):
    row_total, col_count = queries.shape
    head_count = col_count // head_size
    block_rows = min(512, row_total)
    score_scale = 1.0 / math.sqrt(head_size)

    def split_heads(matrix):
        return matrix.reshape(row_total, head_count, head_size).transpose(1, 0, 2)

    def one_head(triple):
        head_query, head_key, head_value = triple
        blocked = head_query.reshape(row_total // block_rows, block_rows, head_size)

        def one_block(query_block):
            scores = jnp.dot(query_block, head_key.T, preferred_element_type=jnp.float32) * score_scale
            row_top = lax.optimization_barrier(jnp.max(scores, axis=-1, keepdims=True))
            raised = jnp.exp(scores - row_top)
            weights = (raised / lax.optimization_barrier(jnp.sum(raised, axis=-1, keepdims=True))).astype(jnp.bfloat16)
            return jnp.dot(weights, head_value, preferred_element_type=jnp.float32).astype(jnp.bfloat16)
        return lax.map(one_block, blocked).reshape(row_total, head_size)
    merged = lax.map(one_head, (split_heads(queries), split_heads(key_rows), split_heads(value_rows)))
    return merged.transpose(1, 0, 2).reshape(row_total, col_count)

def velocity(latent, noise_level, params):
    w_in, w_query, w_key, w_value, w_out, w_final, mod_scale, mod_shift, skip_gain = params
    hidden = jnp.dot(latent.astype(jnp.bfloat16), w_in, preferred_element_type=jnp.float32)
    squares = lax.optimization_barrier(jnp.mean(hidden * hidden, axis=-1, keepdims=True))
    normed = hidden * lax.rsqrt(squares + 1e-06)
    modulated = (normed * (1.0 + noise_level * mod_scale) + noise_level * mod_shift).astype(jnp.bfloat16)
    queries = jnp.dot(modulated, w_query, preferred_element_type=jnp.float32).astype(jnp.bfloat16)
    key_rows = jnp.dot(modulated, w_key, preferred_element_type=jnp.float32).astype(jnp.bfloat16)
    value_rows = jnp.dot(modulated, w_value, preferred_element_type=jnp.float32).astype(jnp.bfloat16)
    attended = attend(queries, key_rows, value_rows, HEAD_SIZE)
    mixed = jnp.dot(attended, w_out, preferred_element_type=jnp.float32) + skip_gain * normed
    return jnp.dot(mixed, w_final, precision=lax.Precision.HIGHEST, preferred_element_type=jnp.float32)

def reference(noise, timesteps, fine_counts, w_in, w_query, w_key, w_value, w_out, w_final, mod_scale, mod_shift, skip_gain):
    params = (w_in, w_query, w_key, w_value, w_out, w_final, mod_scale, mod_shift, skip_gain)
    sigmas = timesteps.astype(jnp.float32) / 1000.0
    columns = jnp.arange(FINE_MAX + 1).astype(jnp.int32)

    def coarse(latent, slab_id):
        final_level = jnp.sum(jnp.where(columns == fine_counts[slab_id], sigmas[slab_id], 0.0))
        return latent + (final_level - sigmas[slab_id, 0]) * velocity(latent, sigmas[slab_id, 0], params)

    def fine(latent, slab_id):
        for fine_step in range(FINE_MAX):
            step_size = jnp.where(fine_step < fine_counts[slab_id], sigmas[slab_id, fine_step + 1] - sigmas[slab_id, fine_step], 0.0)
            latent = latent + step_size * velocity(latent, sigmas[slab_id, fine_step], params)
        return latent
    first_coarse = coarse(noise, 0)
    starts = [noise]
    for slab_id in range(N_SLAB - 1):
        starts.append(first_coarse if slab_id == 0 else coarse(starts[slab_id], slab_id))
    slab_list = []
    for outer in range(ITERS):
        corrections = []
        for slab_id in range(N_SLAB):
            coarse_old = first_coarse if slab_id == 0 else coarse(starts[slab_id], slab_id)
            corrections.append(fine(starts[slab_id], slab_id) - coarse_old)
        fresh = [noise]
        slab_list = []
        for slab_id in range(N_SLAB):
            coarse_new = first_coarse if slab_id == 0 else coarse(fresh[slab_id], slab_id)
            ended = coarse_new + corrections[slab_id]
            slab_list.append(ended)
            if slab_id + 1 < N_SLAB:
                fresh.append(ended)
        starts = fresh
    return jnp.stack(slab_list)
```

```python
import functools
import math

import jax
import jax.numpy as jnp
from jax import lax
from jax.experimental import pallas as pl
from jax.experimental.pallas import tpu as pltpu
from jax.sharding import PartitionSpec as P

HEAD_SIZE = 128
F32 = jnp.float32
BF16 = jnp.bfloat16
NT = (((1,), (1,)), ((), ()))
TN = (((0,), (0,)), ((), ()))


def dot(a, b, dims=None, precision=None):
    if dims is None:
        dims = (((1,), (0,)), ((), ()))
    return lax.dot_general(a, b, dims, precision=precision, preferred_element_type=F32)


def split2(x):
    high = x.astype(BF16)
    return high, (x - high.astype(F32)).astype(BF16)


def split3(x):
    high, _ = split2(x)
    rest = x - high.astype(F32)
    mid, low = split2(rest)
    return high, mid, low


def dot_fine(a, b):
    a_high, a_low = split2(a)
    b_high, b_low = split2(b)
    return dot(
        jnp.concatenate([a_high, a_high, a_low], axis=1),
        jnp.concatenate([b_high, b_low, b_high], axis=1),
        NT,
    )


def payload_rows(channels):
    return channels + channels // 2 + 16


def fold_kernel(
    noise_ref,
    w_in_hbm,
    wq_hbm,
    wk_hbm,
    wv_hbm,
    wo_hbm,
    wf_hbm,
    scale_ref,
    shift_ref,
    out_ref,
    w_in,
    lift,
    w_a,
    w_b,
    wo,
    wf,
    wf2,
    sems,
    *,
    chunks,
):
    slab = lax.axis_index("slab")
    channels, width = w_in.shape
    depth = width // chunks
    half = channels // 2

    def fetch(src, dst, index):
        copy = pltpu.make_async_copy(src, dst, sems.at[index])
        copy.start()
        return copy

    def build_lift():
        base = w_in[...].astype(F32)
        high, low = split2(base * scale_ref[...])
        lift[0:channels] = w_in[...]
        lift[channels : 2 * channels] = high
        lift[2 * channels : 3 * channels] = low
        shift_high, shift_low = split2(shift_ref[...])
        row = lax.broadcasted_iota(jnp.int32, (16, width), 0)
        tail = jnp.where(
            row == 0,
            shift_high.astype(F32),
            jnp.where(row == 1, shift_low.astype(F32), 0.0),
        )
        lift[3 * channels : 3 * channels + 16] = tail.astype(BF16)

    def parts(total):
        first = total[0:channels]
        second = total[channels : 2 * channels] + total[2 * channels : 3 * channels]
        tail = total[3 * channels : 3 * channels + 8]
        third = tail[0:1] + tail[1:2]
        return first, second, third

    def zero_rows(count):
        return jnp.zeros((count, 2 * channels), F32)

    @pl.when(slab == 0)
    def _():
        first = fetch(w_in_hbm, w_in, 0)
        copies = []
        for c in range(chunks):
            rows = pl.ds(c * depth, depth)
            copies.append(
                (
                    fetch(wq_hbm.at[rows], w_a.at[rows], 1 + 2 * c),
                    fetch(wk_hbm.at[rows], w_b.at[rows], 2 + 2 * c),
                )
            )
        first.wait()
        build_lift()
        total = None
        for c in range(chunks):
            rows = slice(c * depth, (c + 1) * depth)
            for copy in copies[c]:
                copy.wait()
            term = dot(lift[:, rows], jnp.concatenate([w_a[rows], w_b[rows]], axis=1))
            total = term if total is None else total + term
        q0, q1, q2 = parts(total[:, 0:HEAD_SIZE] * (1.0 / math.sqrt(HEAD_SIZE)))
        k0, k1, k2 = parts(total[:, HEAD_SIZE : 2 * HEAD_SIZE])
        pad = jnp.zeros((7, HEAD_SIZE), F32)
        q_all = jnp.concatenate([q0, q1], axis=0)
        k_all = jnp.concatenate([k0, k1], axis=0)
        form = dot_fine(k_all, q_all)
        k_last = jnp.concatenate([k2, pad], axis=0)
        q_last = jnp.concatenate([q2, pad], axis=0)
        a_rows = dot_fine(k_last, q_all)[0:1]
        b_rows = dot_fine(q_last, k_all)[0:1]
        constant = jnp.sum(k2 * q2)
        lane = lax.broadcasted_iota(jnp.int32, (channels, 2 * channels), 1)
        top, bottom = form[0:channels], form[channels : 2 * channels]
        rolled = pltpu.roll(bottom, channels, 1)
        out_ref[0:channels] = jnp.where(lane < channels, top, top + rolled).astype(BF16)
        out_ref[channels : channels + half] = jnp.where(
            lane[0:half] < channels, rolled[0:half], bottom[half:channels]
        ).astype(BF16)
        lane = lax.broadcasted_iota(jnp.int32, (16, 2 * channels), 1)
        row = lax.broadcasted_iota(jnp.int32, (16, 2 * channels), 0)
        a_roll = pltpu.roll(jnp.broadcast_to(a_rows, (8, 2 * channels)), channels, 1)[0:1]
        b_roll = pltpu.roll(jnp.broadcast_to(b_rows, (8, 2 * channels)), channels, 1)[0:1]
        left = lane < channels
        tile_one = jnp.where(left, 0.0, a_roll)
        tile_two = jnp.where(left, a_roll, 0.0)
        at_const = (lane == channels + 2) | (lane == channels + 3)
        tile_two = jnp.where(at_const, constant, tile_two)
        ext = jnp.where(
            row == 0,
            tile_one,
            jnp.where(
                row == 1,
                tile_two,
                jnp.where(row == 2, b_rows, jnp.where(row == 3, b_roll, 0.0)),
            ),
        )
        out_ref[channels + half : channels + half + 16] = ext.astype(BF16)

    @pl.when(slab != 0)
    def _():
        first = fetch(w_in_hbm, w_in, 0)
        second = fetch(wf_hbm, wf, 1)
        third = fetch(wo_hbm, wo, 2)
        copies = []
        for c in range(chunks):
            rows = pl.ds(c * depth, depth)
            copies.append(fetch(wv_hbm.at[rows], w_a.at[rows], 3 + c))
        first.wait()
        build_lift()
        second.wait()
        high, low = split2(wf[...])
        wf2[0:channels] = high
        wf2[channels : 2 * channels] = low
        third.wait()
        both = dot(wf2[...], wo[...], NT)
        out_t = both[0:channels] + both[channels : 2 * channels]
        total = None
        for c in range(chunks):
            rows = slice(c * depth, (c + 1) * depth)
            copies[c].wait()
            term = dot(lift[:, rows], w_a[rows])
            total = term if total is None else total + term
        v0, v1, v2 = parts(total)
        out_ref[0:channels] = dot_fine(out_t, jnp.concatenate([v0, v1], axis=0)).astype(BF16)
        v_last = jnp.concatenate([v2, jnp.zeros((7, HEAD_SIZE), F32)], axis=0)
        p_row = dot_fine(v_last, jnp.concatenate([out_t, out_t], axis=0))[0:1]
        row = lax.broadcasted_iota(jnp.int32, (16, 2 * channels), 0)
        out_ref[channels : channels + 16] = jnp.where(row == 0, p_row, 0.0).astype(BF16)
        tokens = noise_ref.shape[0]
        n_high, n_mid, n_low = split3(noise_ref[...])
        pieces = jnp.concatenate(
            [
                jnp.concatenate([n_high.astype(F32), n_mid.astype(F32)], axis=1),
                jnp.concatenate([n_low.astype(F32), jnp.zeros_like(noise_ref[...])], axis=1),
            ],
            axis=0,
        )
        out_ref[channels + 16 : channels + 16 + 2 * tokens] = pieces.astype(BF16)


def side_kernel(w_in_ref, wf_ref, gain_ref, out_ref):
    channels, width = w_in_ref.shape
    w_in = w_in_ref[...]
    gram = dot(w_in, w_in, NT) * (1.0 / width)
    g_high, g_mid, g_low = split3(gram)
    gained = w_in.astype(F32) * gain_ref[...]
    s_high, s_low = split2(dot_fine(wf_ref[...], gained))
    out_ref[...] = jnp.concatenate([g_high, g_mid, g_low, s_high, s_low], axis=0)


def solve_kernel(
    times_ref,
    counts_ref,
    noise_ref,
    own_ref,
    other_ref,
    side_ref,
    out_ref,
    t1,
    t2,
    t3,
    a1,
    a2,
    start,
    *,
    heads,
):
    slab = lax.axis_index("slab")
    tokens, channels = noise_ref.shape
    count = start.shape[1]
    lanes = 2 * count
    half = channels // 2
    rows = payload_rows(channels)
    fine_most = times_ref.shape[1] - 1
    first_slab = slab == 0

    wide = lax.broadcasted_iota(jnp.int32, (channels, 2 * channels), 1)
    sel_row = lax.broadcasted_iota(jnp.int32, (16, 2 * channels), 0)
    sel_lane = lax.broadcasted_iota(jnp.int32, (16, 2 * channels), 1) - channels

    def pick(cond):
        return jnp.where(cond, 1.0, 0.0).astype(BF16)

    b_pick = pick(
        ((sel_row == 2) & ((sel_lane == 0) | (sel_lane == 1)))
        | ((sel_row == 3) & ((sel_lane == 2) | (sel_lane == 3)))
    )
    p_pick = pick((sel_row == 0) & ((sel_lane == 4) | (sel_lane == 5)))
    for h in range(heads):
        base = h * rows

        def score_side(lo, n):
            at = pl.ds(base + lo, n)
            return jnp.where(first_slab, own_ref[at].astype(F32), other_ref[at].astype(F32))

        def value_side(lo, n):
            at = pl.ds(base + lo, n)
            return jnp.where(first_slab, other_ref[at].astype(F32), own_ref[at].astype(F32))

        to = pl.ds(h * channels, channels)
        t1[to] = score_side(0, channels).astype(BF16)
        folded = score_side(channels, half)
        square = jnp.concatenate([folded, pltpu.roll(folded, channels, 1)], axis=0)
        ext = score_side(channels + half, 16)
        p_ext = value_side(channels, 16)
        columns = dot(ext[:, 0:channels].astype(BF16), b_pick, TN) + dot(
            p_ext[:, 0:channels].astype(BF16), p_pick, TN
        )
        t2[to] = jnp.where(wide < channels, square, columns).astype(BF16)
        a1[h : h + 1] = ext[0:1]
        a2[h : h + 1] = ext[1:2]
        t3[to] = value_side(0, channels).astype(BF16)
        pieces = value_side(channels + 16, 2 * tokens)
        upper, lower = pieces[0:tokens], pieces[tokens : 2 * tokens]
        whole = (upper + pltpu.roll(upper, channels, 1)) + lower
        start[:, pl.ds(h * tokens, tokens)] = jnp.transpose(whole)[0:channels]

    lane = lax.broadcasted_iota(jnp.int32, (1, lanes), 1)
    left = lane < count

    def level(slab_id, column):
        return (jnp.zeros((1, lanes), jnp.int32) + times_ref[slab_id, column]).astype(F32) / 1000.0

    def step(slab_id, j):
        size = level(slab_id, j + 1) - level(slab_id, j)
        return jnp.where(j < counts_ref[slab_id], size, 0.0)

    def span(slab_id):
        last = jnp.zeros((1, lanes), F32)
        for column in range(fine_most + 1):
            last = jnp.where(column == counts_ref[slab_id], level(slab_id, column), last)
        return last - level(slab_id, 0)

    def velocity(u, s):
        rounded = u.astype(BF16)
        sides = dot(side_ref[...], rounded)
        form = (
            sides[0:channels] + sides[channels : 2 * channels]
        ) + sides[2 * channels : 3 * channels]
        squares = jnp.sum(form * rounded.astype(F32), axis=0, keepdims=True)
        r = lax.rsqrt(jnp.maximum(squares, 0.0) + 1e-06)
        skip = r * (sides[3 * channels : 4 * channels] + sides[4 * channels : 5 * channels])
        x = r * rounded.astype(F32)
        s2 = s * s
        s_high, s_low = split2(s)
        s2_high, s2_low = split2(s2)
        row = lax.broadcasted_iota(jnp.int32, (channels, lanes), 0)
        s_rows = jnp.where(
            row == 0,
            s_high.astype(F32),
            jnp.where(
                row == 1,
                s_low.astype(F32),
                jnp.where(
                    row == 2, s2_high.astype(F32), jnp.where(row == 3, s2_low.astype(F32), 0.0)
                ),
            ),
        )
        p_rows = jnp.where(
            row == 4, s_high.astype(F32), jnp.where(row == 5, s_low.astype(F32), 0.0)
        )
        x_one = jnp.concatenate([x, s * x], axis=0).astype(BF16)
        x_two = jnp.concatenate([s2 * x, s_rows], axis=0).astype(BF16)
        x_p = jnp.concatenate([jnp.zeros_like(x), p_rows], axis=0).astype(BF16)
        query = (dot(t1[...], x_one) + dot(t2[...], x_two)).astype(BF16)
        value = (dot(t3[...], x_one) + dot(t2[...], x_p)).astype(BF16)
        column_terms = dot(a1[...].astype(BF16), x_one) + dot(a2[...].astype(BF16), x_two)
        keys = jnp.transpose(x).astype(BF16)
        lhs, rhs = [], []
        for h in range(heads):
            at = slice(h * channels, (h + 1) * channels)
            both = dot(keys, query[at])
            scores = jnp.where(left, both[0:count], both[count:lanes]) + column_terms[h : h + 1]
            raised = jnp.exp(scores - jnp.max(scores, axis=0, keepdims=True))
            weights = raised / jnp.sum(raised, axis=0, keepdims=True)
            lhs.append(value[at])
            rhs.append(jnp.where(left, weights, 0.0).astype(BF16))
            rhs.append(jnp.where(left, 0.0, weights).astype(BF16))
        return skip + dot(jnp.concatenate(lhs, axis=1), jnp.concatenate(rhs, axis=0))

    noise = jnp.concatenate([start[...], start[...]], axis=1)
    moved = velocity(noise, level(0, 0))
    first_coarse = noise + span(0) * moved
    u = jnp.where(left, noise + step(0, 0) * moved, first_coarse)
    coarse_old = None
    for j in range(fine_most):
        last = j == fine_most - 1
        s = jnp.where(left, level(1, 0) if last else level(0, j + 1), level(1, j))
        moved = velocity(u, s)
        if j == 0:
            coarse_old = u + span(1) * moved
        ahead = span(1) if last else step(0, j + 1)
        if last:
            fine_first = u
        u = u + jnp.where(left, ahead, step(1, j)) * moved
    change = pltpu.roll(u - coarse_old, count, 1)
    end_second = u + change
    end_first = first_coarse + (fine_first - first_coarse)
    ended = jnp.where(first_slab, end_first, end_second)
    out_ref[...] = jnp.transpose(ended)[0:tokens]


def gathered(value, axis):
    size = lax.axis_size(axis)
    stride = size // 2
    while stride:
        pairs = [(i, i ^ stride) for i in range(size)]
        value = jnp.concatenate([value, lax.ppermute(value, axis, pairs)], axis=0)
        stride //= 2
    return value


def local(
    noise,
    timesteps,
    fine_counts,
    w_in,
    w_query,
    w_key,
    w_value,
    w_out,
    w_final,
    mod_scale,
    mod_shift,
    skip_gain,
):
    channels, width = w_in.shape
    tokens = noise.shape[0]
    heads = lax.axis_size("seq")
    count = tokens * heads
    rows = payload_rows(channels)
    wf_t = w_final.T
    row_of = lambda vector: vector.reshape(1, width)
    vmem = pl.BlockSpec(memory_space=pltpu.VMEM)
    smem = pl.BlockSpec(memory_space=pltpu.SMEM)
    hbm = pl.BlockSpec(memory_space=pl.ANY)
    chunks = 5
    packed = pl.pallas_call(
        functools.partial(fold_kernel, chunks=chunks),
        out_shape=jax.ShapeDtypeStruct((rows, 2 * channels), BF16),
        in_specs=[vmem, hbm, hbm, hbm, hbm, hbm, hbm, vmem, vmem],
        out_specs=vmem,
        scratch_shapes=[
            pltpu.VMEM((channels, width), BF16),
            pltpu.VMEM((3 * channels + 16, width), BF16),
            pltpu.VMEM((width, HEAD_SIZE), BF16),
            pltpu.VMEM((width, HEAD_SIZE), BF16),
            pltpu.VMEM((HEAD_SIZE, width), BF16),
            pltpu.VMEM((channels, width), F32),
            pltpu.VMEM((2 * channels, width), BF16),
            pltpu.SemaphoreType.DMA((2 * chunks + 4,)),
        ],
        name="fold",
    )(noise, w_in, w_query, w_key, w_value, w_out, wf_t, row_of(mod_scale), row_of(mod_shift))
    side = pl.pallas_call(
        side_kernel,
        out_shape=jax.ShapeDtypeStruct((5 * channels, channels), BF16),
        in_specs=[vmem, vmem, vmem],
        out_specs=vmem,
        name="side",
    )(w_in, wf_t, row_of(skip_gain))
    own = gathered(packed, "seq")
    other = lax.ppermute(own, "slab", [(0, 1), (1, 0)])
    ended = pl.pallas_call(
        functools.partial(solve_kernel, heads=heads),
        out_shape=jax.ShapeDtypeStruct((tokens, channels), F32),
        in_specs=[smem, smem, vmem, vmem, vmem, vmem],
        out_specs=vmem,
        scratch_shapes=[
            pltpu.VMEM((heads * channels, 2 * channels), BF16),
            pltpu.VMEM((heads * channels, 2 * channels), BF16),
            pltpu.VMEM((heads * channels, 2 * channels), BF16),
            pltpu.VMEM((heads, 2 * channels), F32),
            pltpu.VMEM((heads, 2 * channels), F32),
            pltpu.VMEM((channels, count), F32),
        ],
        name="solve",
    )(timesteps, fine_counts, noise, own, other, side)
    return ended[None]


def solution(mesh):
    placed = (
        P(("groups", "seq"), None),
        P("groups", None),
        P("groups"),
        P(),
        P(None, "seq"),
        P(None, "seq"),
        P(None, "seq"),
        P("seq", None),
        P(),
        P(),
        P(),
        P(),
    )
    return jax.shard_map(
        local,
        mesh=mesh,
        in_specs=placed,
        out_specs=P("slab", ("groups", "seq"), None),
        check_vma=False,
    )
```

```python
import functools
import math

import jax
import jax.numpy as jnp
from jax import lax
from jax.experimental import pallas as pl
from jax.experimental.pallas import tpu as pltpu
from jax.sharding import PartitionSpec as P

HEAD_SIZE = 128
F32 = jnp.float32
BF16 = jnp.bfloat16
NT = (((1,), (1,)), ((), ()))
TN = (((0,), (0,)), ((), ()))


def dot(a, b, dims=None, precision=None):
    if dims is None:
        dims = (((1,), (0,)), ((), ()))
    return lax.dot_general(a, b, dims, precision=precision, preferred_element_type=F32)


def split2(x):
    high = x.astype(BF16)
    return high, (x - high.astype(F32)).astype(BF16)


def split3(x):
    high, _ = split2(x)
    rest = x - high.astype(F32)
    mid, low = split2(rest)
    return high, mid, low


def dot_fine(a, b):
    a_high, a_low = split2(a)
    b_high, b_low = split2(b)
    return dot(
        jnp.concatenate([a_high, a_high, a_low], axis=1),
        jnp.concatenate([b_high, b_low, b_high], axis=1),
        NT,
    )


def payload_rows(channels):
    return channels + channels // 2 + 16


def fold_kernel(
    noise_ref,
    w_in_hbm,
    wq_hbm,
    wk_hbm,
    wv_hbm,
    wo_hbm,
    wf_hbm,
    scale_ref,
    shift_ref,
    out_ref,
    w_in,
    lift,
    w_a,
    w_b,
    wo,
    wf,
    wf2,
    sems,
    *,
    chunks,
):
    slab = lax.axis_index("slab")
    channels, width = w_in.shape
    depth = width // chunks
    half = channels // 2

    def fetch(src, dst, index):
        copy = pltpu.make_async_copy(src, dst, sems.at[index])
        copy.start()
        return copy

    def build_lift():
        base = w_in[...].astype(F32)
        high, low = split2(base * scale_ref[...].reshape(1, width))
        lift[0:channels] = w_in[...]
        lift[channels : 2 * channels] = high
        lift[2 * channels : 3 * channels] = low
        shift_high, shift_low = split2(shift_ref[...].reshape(1, width))
        row = lax.broadcasted_iota(jnp.int32, (16, width), 0)
        tail = jnp.where(
            row == 0,
            shift_high.astype(F32),
            jnp.where(row == 1, shift_low.astype(F32), 0.0),
        )
        lift[3 * channels : 3 * channels + 16] = tail.astype(BF16)

    def parts(total):
        first = total[0:channels]
        second = total[channels : 2 * channels] + total[2 * channels : 3 * channels]
        tail = total[3 * channels : 3 * channels + 8]
        third = tail[0:1] + tail[1:2]
        return first, second, third

    def zero_rows(count):
        return jnp.zeros((count, 2 * channels), F32)

    @pl.when(slab == 0)
    def _():
        first = fetch(w_in_hbm, w_in, 0)
        copies = []
        for c in range(chunks):
            rows = pl.ds(c * depth, depth)
            copies.append(
                (
                    fetch(wq_hbm.at[rows], w_a.at[rows], 1 + 2 * c),
                    fetch(wk_hbm.at[rows], w_b.at[rows], 2 + 2 * c),
                )
            )
        first.wait()
        build_lift()
        total = None
        for c in range(chunks):
            rows = slice(c * depth, (c + 1) * depth)
            for copy in copies[c]:
                copy.wait()
            term = dot(lift[:, rows], jnp.concatenate([w_a[rows], w_b[rows]], axis=1))
            total = term if total is None else total + term
        q0, q1, q2 = parts(total[:, 0:HEAD_SIZE] * (1.0 / math.sqrt(HEAD_SIZE)))
        k0, k1, k2 = parts(total[:, HEAD_SIZE : 2 * HEAD_SIZE])
        pad = jnp.zeros((7, HEAD_SIZE), F32)
        q_all = jnp.concatenate([q0, q1], axis=0)
        k_all = jnp.concatenate([k0, k1], axis=0)
        form = dot_fine(k_all, q_all)
        k_last = jnp.concatenate([k2, pad], axis=0)
        q_last = jnp.concatenate([q2, pad], axis=0)
        a_rows = dot_fine(k_last, q_all)[0:1]
        b_rows = dot_fine(q_last, k_all)[0:1]
        constant = jnp.sum(k2 * q2)
        lane = lax.broadcasted_iota(jnp.int32, (channels, 2 * channels), 1)
        top, bottom = form[0:channels], form[channels : 2 * channels]
        rolled = pltpu.roll(bottom, channels, 1)
        out_ref[0:channels] = jnp.where(lane < channels, top, top + rolled).astype(BF16)
        out_ref[channels : channels + half] = jnp.where(
            lane[0:half] < channels, rolled[0:half], bottom[half:channels]
        ).astype(BF16)
        lane = lax.broadcasted_iota(jnp.int32, (16, 2 * channels), 1)
        row = lax.broadcasted_iota(jnp.int32, (16, 2 * channels), 0)
        a_roll = pltpu.roll(jnp.broadcast_to(a_rows, (8, 2 * channels)), channels, 1)[0:1]
        b_roll = pltpu.roll(jnp.broadcast_to(b_rows, (8, 2 * channels)), channels, 1)[0:1]
        left = lane < channels
        tile_one = jnp.where(left, 0.0, a_roll)
        tile_two = jnp.where(left, a_roll, 0.0)
        at_const = (lane == channels + 2) | (lane == channels + 3)
        tile_two = jnp.where(at_const, constant, tile_two)
        ext = jnp.where(
            row == 0,
            tile_one,
            jnp.where(
                row == 1,
                tile_two,
                jnp.where(row == 2, b_rows, jnp.where(row == 3, b_roll, 0.0)),
            ),
        )
        out_ref[channels + half : channels + half + 16] = ext.astype(BF16)

    @pl.when(slab != 0)
    def _():
        first = fetch(w_in_hbm, w_in, 0)
        second = fetch(wf_hbm, wf, 1)
        third = fetch(wo_hbm, wo, 2)
        copies = []
        for c in range(chunks):
            rows = pl.ds(c * depth, depth)
            copies.append(fetch(wv_hbm.at[rows], w_a.at[rows], 3 + c))
        first.wait()
        build_lift()
        second.wait()
        high, low = split2(wf[...])
        wf2[0:channels] = high
        wf2[channels : 2 * channels] = low
        third.wait()
        both = dot(wf2[...], wo[...], NT)
        out_t = both[0:channels] + both[channels : 2 * channels]
        total = None
        for c in range(chunks):
            rows = slice(c * depth, (c + 1) * depth)
            copies[c].wait()
            term = dot(lift[:, rows], w_a[rows])
            total = term if total is None else total + term
        v0, v1, v2 = parts(total)
        out_ref[0:channels] = dot_fine(out_t, jnp.concatenate([v0, v1], axis=0)).astype(BF16)
        v_last = jnp.concatenate([v2, jnp.zeros((7, HEAD_SIZE), F32)], axis=0)
        p_row = dot_fine(v_last, jnp.concatenate([out_t, out_t], axis=0))[0:1]
        row = lax.broadcasted_iota(jnp.int32, (16, 2 * channels), 0)
        out_ref[channels : channels + 16] = jnp.where(row == 0, p_row, 0.0).astype(BF16)
        tokens = noise_ref.shape[0]
        n_high, n_mid, n_low = split3(noise_ref[...])
        pieces = jnp.concatenate(
            [
                jnp.concatenate([n_high.astype(F32), n_mid.astype(F32)], axis=1),
                jnp.concatenate([n_low.astype(F32), jnp.zeros_like(noise_ref[...])], axis=1),
            ],
            axis=0,
        )
        out_ref[channels + 16 : channels + 16 + 2 * tokens] = pieces.astype(BF16)


def side_kernel(w_in_ref, wf_ref, gain_ref, out_ref):
    channels, width = w_in_ref.shape
    w_in = w_in_ref[...]
    gram = dot(w_in, w_in, NT) * (1.0 / width)
    g_high, g_mid, g_low = split3(gram)
    gained = w_in.astype(F32) * gain_ref[...].reshape(1, width)
    s_high, s_low = split2(dot_fine(wf_ref[...], gained))
    out_ref[...] = jnp.concatenate([g_high, g_mid, g_low, s_high, s_low], axis=0)


def solve_kernel(
    times_ref,
    counts_ref,
    noise_ref,
    own_ref,
    other_ref,
    side_ref,
    out_ref,
    t1,
    t2,
    t3,
    a1,
    a2,
    start,
    *,
    heads,
):
    slab = lax.axis_index("slab")
    tokens, channels = noise_ref.shape
    count = start.shape[1]
    lanes = 2 * count
    half = channels // 2
    rows = payload_rows(channels)
    fine_most = times_ref.shape[1] - 1
    first_slab = slab == 0

    wide = lax.broadcasted_iota(jnp.int32, (channels, 2 * channels), 1)
    sel_row = lax.broadcasted_iota(jnp.int32, (16, 2 * channels), 0)
    sel_lane = lax.broadcasted_iota(jnp.int32, (16, 2 * channels), 1) - channels

    def pick(cond):
        return jnp.where(cond, 1.0, 0.0).astype(BF16)

    b_pick = pick(
        ((sel_row == 2) & ((sel_lane == 0) | (sel_lane == 1)))
        | ((sel_row == 3) & ((sel_lane == 2) | (sel_lane == 3)))
    )
    p_pick = pick((sel_row == 0) & ((sel_lane == 4) | (sel_lane == 5)))
    for h in range(heads):
        base = h * rows

        def score_side(lo, n):
            at = pl.ds(base + lo, n)
            return jnp.where(first_slab, own_ref[at].astype(F32), other_ref[at].astype(F32))

        def value_side(lo, n):
            at = pl.ds(base + lo, n)
            return jnp.where(first_slab, other_ref[at].astype(F32), own_ref[at].astype(F32))

        to = pl.ds(h * channels, channels)
        t1[to] = score_side(0, channels).astype(BF16)
        folded = score_side(channels, half)
        square = jnp.concatenate([folded, pltpu.roll(folded, channels, 1)], axis=0)
        ext = score_side(channels + half, 16)
        p_ext = value_side(channels, 16)
        columns = dot(ext[:, 0:channels].astype(BF16), b_pick, TN) + dot(
            p_ext[:, 0:channels].astype(BF16), p_pick, TN
        )
        t2[to] = jnp.where(wide < channels, square, columns).astype(BF16)
        a1[h : h + 1] = ext[0:1]
        a2[h : h + 1] = ext[1:2]
        t3[to] = value_side(0, channels).astype(BF16)
        pieces = value_side(channels + 16, 2 * tokens)
        upper, lower = pieces[0:tokens], pieces[tokens : 2 * tokens]
        whole = (upper + pltpu.roll(upper, channels, 1)) + lower
        start[:, pl.ds(h * tokens, tokens)] = jnp.transpose(whole)[0:channels]

    lane = lax.broadcasted_iota(jnp.int32, (1, lanes), 1)
    left = lane < count

    def level(slab_id, column):
        return (jnp.zeros((1, lanes), jnp.int32) + times_ref[slab_id, column]).astype(F32) / 1000.0

    def step(slab_id, j):
        size = level(slab_id, j + 1) - level(slab_id, j)
        return jnp.where(j < counts_ref[slab_id], size, 0.0)

    def span(slab_id):
        last = jnp.zeros((1, lanes), F32)
        for column in range(fine_most + 1):
            last = jnp.where(column == counts_ref[slab_id], level(slab_id, column), last)
        return last - level(slab_id, 0)

    def velocity(u, s):
        rounded = u.astype(BF16)
        sides = dot(side_ref[...], rounded)
        form = (
            sides[0:channels] + sides[channels : 2 * channels]
        ) + sides[2 * channels : 3 * channels]
        squares = jnp.sum(form * rounded.astype(F32), axis=0, keepdims=True)
        r = lax.rsqrt(jnp.maximum(squares, 0.0) + 1e-06)
        skip = r * (sides[3 * channels : 4 * channels] + sides[4 * channels : 5 * channels])
        x = r * rounded.astype(F32)
        s2 = s * s
        s_high, s_low = split2(s)
        s2_high, s2_low = split2(s2)
        row = lax.broadcasted_iota(jnp.int32, (channels, lanes), 0)
        s_rows = jnp.where(
            row == 0,
            s_high.astype(F32),
            jnp.where(
                row == 1,
                s_low.astype(F32),
                jnp.where(
                    row == 2, s2_high.astype(F32), jnp.where(row == 3, s2_low.astype(F32), 0.0)
                ),
            ),
        )
        p_rows = jnp.where(
            row == 4, s_high.astype(F32), jnp.where(row == 5, s_low.astype(F32), 0.0)
        )
        x_one = jnp.concatenate([x, s * x], axis=0).astype(BF16)
        x_two = jnp.concatenate([s2 * x, s_rows], axis=0).astype(BF16)
        x_p = jnp.concatenate([jnp.zeros_like(x), p_rows], axis=0).astype(BF16)
        query = (dot(t1[...], x_one) + dot(t2[...], x_two)).astype(BF16)
        value = (dot(t3[...], x_one) + dot(t2[...], x_p)).astype(BF16)
        column_terms = dot(a1[...].astype(BF16), x_one) + dot(a2[...].astype(BF16), x_two)
        keys = jnp.transpose(x).astype(BF16)
        lhs, rhs = [], []
        for h in range(heads):
            at = slice(h * channels, (h + 1) * channels)
            both = dot(keys, query[at])
            scores = jnp.where(left, both[0:count], both[count:lanes]) + column_terms[h : h + 1]
            raised = jnp.exp(scores - jnp.max(scores, axis=0, keepdims=True))
            weights = raised / jnp.sum(raised, axis=0, keepdims=True)
            lhs.append(value[at])
            rhs.append(jnp.where(left, weights, 0.0).astype(BF16))
            rhs.append(jnp.where(left, 0.0, weights).astype(BF16))
        return skip + dot(jnp.concatenate(lhs, axis=1), jnp.concatenate(rhs, axis=0))

    noise = jnp.concatenate([start[...], start[...]], axis=1)
    moved = velocity(noise, level(0, 0))
    first_coarse = noise + span(0) * moved
    u = jnp.where(left, noise + step(0, 0) * moved, first_coarse)
    coarse_old = None
    for j in range(fine_most):
        last = j == fine_most - 1
        s = jnp.where(left, level(1, 0) if last else level(0, j + 1), level(1, j))
        moved = velocity(u, s)
        if j == 0:
            coarse_old = u + span(1) * moved
        ahead = span(1) if last else step(0, j + 1)
        if last:
            fine_first = u
        u = u + jnp.where(left, ahead, step(1, j)) * moved
    change = pltpu.roll(u - coarse_old, count, 1)
    end_second = u + change
    end_first = first_coarse + (fine_first - first_coarse)
    ended = jnp.where(first_slab, end_first, end_second)
    out_ref[...] = jnp.transpose(ended)[0:tokens]


def gathered(value, axis):
    size = lax.axis_size(axis)
    stride = size // 2
    while stride:
        pairs = [(i, i ^ stride) for i in range(size)]
        value = jnp.concatenate([value, lax.ppermute(value, axis, pairs)], axis=0)
        stride //= 2
    return value


def local(
    noise,
    timesteps,
    fine_counts,
    w_in,
    w_query,
    w_key,
    w_value,
    w_out,
    w_final,
    mod_scale,
    mod_shift,
    skip_gain,
):
    channels, width = w_in.shape
    tokens = noise.shape[0]
    heads = lax.axis_size("seq")
    count = tokens * heads
    rows = payload_rows(channels)
    wf_t = w_final.T
    vmem = pl.BlockSpec(memory_space=pltpu.VMEM)
    smem = pl.BlockSpec(memory_space=pltpu.SMEM)
    hbm = pl.BlockSpec(memory_space=pl.ANY)
    chunks = 5
    packed = pl.pallas_call(
        functools.partial(fold_kernel, chunks=chunks),
        out_shape=pltpu.VMEM((rows, 2 * channels), BF16),
        in_specs=[vmem, hbm, hbm, hbm, hbm, hbm, hbm, vmem, vmem],
        out_specs=vmem,
        scratch_shapes=[
            pltpu.VMEM((channels, width), BF16),
            pltpu.VMEM((3 * channels + 16, width), BF16),
            pltpu.VMEM((width, HEAD_SIZE), BF16),
            pltpu.VMEM((width, HEAD_SIZE), BF16),
            pltpu.VMEM((HEAD_SIZE, width), BF16),
            pltpu.VMEM((channels, width), F32),
            pltpu.VMEM((2 * channels, width), BF16),
            pltpu.SemaphoreType.DMA((2 * chunks + 4,)),
        ],
        name="fold",
    )(noise, w_in, w_query, w_key, w_value, w_out, wf_t, mod_scale, mod_shift)
    side = pl.pallas_call(
        side_kernel,
        out_shape=pltpu.VMEM((5 * channels, channels), BF16),
        in_specs=[vmem, vmem, vmem],
        out_specs=vmem,
        name="side",
    )(w_in, wf_t, skip_gain)
    own = gathered(packed, "seq")
    own, side = lax.optimization_barrier((own, side))
    other = lax.ppermute(own, "slab", [(0, 1), (1, 0)])
    own, other, side = (
        pltpu.with_memory_space_constraint(value, pltpu.VMEM) for value in (own, other, side)
    )
    ended = pl.pallas_call(
        functools.partial(solve_kernel, heads=heads),
        out_shape=jax.ShapeDtypeStruct((tokens, channels), F32),
        in_specs=[smem, smem, vmem, vmem, vmem, vmem],
        out_specs=vmem,
        scratch_shapes=[
            pltpu.VMEM((heads * channels, 2 * channels), BF16),
            pltpu.VMEM((heads * channels, 2 * channels), BF16),
            pltpu.VMEM((heads * channels, 2 * channels), BF16),
            pltpu.VMEM((heads, 2 * channels), F32),
            pltpu.VMEM((heads, 2 * channels), F32),
            pltpu.VMEM((channels, count), F32),
        ],
        name="solve",
    )(timesteps, fine_counts, noise, own, other, side)
    return ended[None]


def solution(mesh):
    placed = (
        P(("groups", "seq"), None),
        P("groups", None),
        P("groups"),
        P(),
        P(None, "seq"),
        P(None, "seq"),
        P(None, "seq"),
        P("seq", None),
        P(),
        P(),
        P(),
        P(),
    )
    return jax.shard_map(
        local,
        mesh=mesh,
        in_specs=placed,
        out_specs=P("slab", ("groups", "seq"), None),
        check_vma=False,
    )
```

```python
import functools
import math

import jax
import jax.numpy as jnp
from jax import lax
from jax.experimental import pallas as pl
from jax.experimental.pallas import tpu as pltpu
from jax.sharding import PartitionSpec as P

HEAD_SIZE = 128
F32 = jnp.float32
BF16 = jnp.bfloat16
NT = (((1,), (1,)), ((), ()))
TN = (((0,), (0,)), ((), ()))


def dot(a, b, dims=(((1,), (0,)), ((), ()))):
    return lax.dot_general(a, b, dims, preferred_element_type=F32)


def split2(x):
    high = x.astype(BF16)
    return high, (x - high.astype(F32)).astype(BF16)


def split3(x):
    high = x.astype(BF16)
    mid, low = split2(x - high.astype(F32))
    return high, mid, low


def dot_fine(a, b):
    a_high, a_low = split2(a)
    b_high, b_low = split2(b)
    return dot(
        jnp.concatenate([a_high, a_high, a_low], axis=1),
        jnp.concatenate([b_high, b_low, b_high], axis=1),
        NT,
    )


def layout(channels, tokens):
    second = channels
    third = second + channels // 2
    tail = third + channels
    return second, third, tail, tail + 4 + tokens // 2 + tokens


def iotas(rows, columns):
    return (
        lax.broadcasted_iota(jnp.int32, (rows, columns), 0),
        lax.broadcasted_iota(jnp.int32, (rows, columns), 1),
    )


def fold_kernel(
    noise_ref,
    w_in_hbm,
    wq_hbm,
    wk_hbm,
    wv_hbm,
    wo_hbm,
    wf_hbm,
    scale_ref,
    shift_ref,
    out_ref,
    w_in,
    lift,
    w_a,
    w_b,
    w_c,
    wo,
    wf,
    wf2,
    sems,
    *,
    chunks,
):
    slab = lax.axis_index("slab")
    channels, width = w_in.shape
    depth = width // chunks
    half = channels // 2
    tokens = noise_ref.shape[0]
    second, third, tail, rows_all = layout(channels, tokens)

    def fetch(src, dst, index):
        copy = pltpu.make_async_copy(src, dst, sems.at[index])
        copy.start()
        return copy

    def parts(total):
        last = total[3 * channels : 3 * channels + 8]
        return (
            total[0:channels],
            total[channels : 2 * channels] + total[2 * channels : 3 * channels],
            last[0:1] + last[1:2],
        )

    @pl.when(slab == 0)
    def _():
        out_ref[...] = jnp.zeros_like(out_ref)

    @pl.when(slab != 0)
    def _():
        first = fetch(w_in_hbm, w_in, 0)
        copies = []
        for c in range(chunks):
            at = pl.ds(c * depth, depth)
            copies.append(
                [
                    fetch(src.at[at], dst.at[at], 3 + 3 * c + i)
                    for i, (src, dst) in enumerate(((wq_hbm, w_a), (wk_hbm, w_b), (wv_hbm, w_c)))
                ]
            )
        final_copy = fetch(wf_hbm, wf, 1)
        out_copy = fetch(wo_hbm, wo, 2)
        shift_high, shift_low = split2(shift_ref[...].reshape(1, width))
        row, _ = iotas(16, width)
        lift[3 * channels : 3 * channels + 16] = jnp.where(
            row == 0,
            shift_high.astype(F32),
            jnp.where(row == 1, shift_low.astype(F32), 0.0),
        ).astype(BF16)
        scale = scale_ref[...].reshape(1, width)
        first.wait()
        lift[0:channels] = w_in[...]
        high, low = split2(w_in[...].astype(F32) * scale)
        lift[channels : 2 * channels] = high
        lift[2 * channels : 3 * channels] = low
        total = None
        for c in range(chunks):
            at = slice(c * depth, (c + 1) * depth)
            for copy in copies[c]:
                copy.wait()
            term = dot(lift[:, at], jnp.concatenate([w_a[at], w_b[at], w_c[at]], axis=1))
            total = term if total is None else total + term
        final_copy.wait()
        high, low = split2(wf[...])
        wf2[0:channels] = high
        wf2[channels : 2 * channels] = low
        out_copy.wait()
        both = dot(wf2[...], wo[...], NT)
        out_t = both[0:channels] + both[channels : 2 * channels]
        q0, q1, q2 = parts(total[:, 0:HEAD_SIZE] * (math.log2(math.e) / math.sqrt(HEAD_SIZE)))
        k0, k1, k2 = parts(total[:, HEAD_SIZE : 2 * HEAD_SIZE])
        v0, v1, v2 = parts(total[:, 2 * HEAD_SIZE : 3 * HEAD_SIZE])
        pad = jnp.zeros((7, HEAD_SIZE), F32)
        q_all = jnp.concatenate([q0, q1], axis=0)
        k_all = jnp.concatenate([k0, k1], axis=0)
        form = dot_fine(k_all, q_all)
        a_rows = dot_fine(jnp.concatenate([k2, pad], axis=0), q_all)
        b_rows = dot_fine(jnp.concatenate([q2, pad], axis=0), k_all)
        constant = jnp.sum(k2 * q2)
        p_rows = dot_fine(
            jnp.concatenate([v2, pad], axis=0), jnp.concatenate([out_t, out_t], axis=0)
        )
        _, lane = iotas(channels, 2 * channels)
        top, bottom = form[0:channels], form[channels : 2 * channels]
        rolled = pltpu.roll(bottom, channels, 1)
        out_ref[0:channels] = jnp.where(lane < channels, top, top + rolled).astype(BF16)
        out_ref[second:third] = jnp.where(
            lane[0:half] < channels, rolled[0:half], bottom[half:channels]
        ).astype(BF16)
        out_ref[third:tail] = dot_fine(out_t, jnp.concatenate([v0, v1], axis=0)).astype(BF16)
        n_high, n_mid, n_low = (part.astype(F32) for part in split3(noise_ref[...]))
        lows = jnp.concatenate([n_low[0 : tokens // 2], n_low[tokens // 2 : tokens]], axis=1)
        row, lane = iotas(4, 2 * channels)
        left = lane < channels
        a_roll = pltpu.roll(a_rows, channels, 1)[0:1]
        b_roll = pltpu.roll(b_rows, channels, 1)[0:1]
        at_const = (lane == channels + 2) | (lane == channels + 3)
        vectors = jnp.where(
            row == 0,
            jnp.where(left, 0.0, a_roll),
            jnp.where(
                row == 1,
                jnp.where(left, a_roll, jnp.where(at_const, constant, 0.0)),
                jnp.where(row == 2, jnp.where(left, b_rows[0:1], p_rows[0:1]), b_roll),
            ),
        )
        out_ref[tail:rows_all] = jnp.concatenate(
            [vectors, lows, jnp.concatenate([n_high, n_mid], axis=1)], axis=0
        ).astype(BF16)


def unpack(pay_ref, base, h, t2, t2z, a1, a2, start, channels, tokens):
    second, third, tail, rows_all = layout(channels, tokens)
    folded = pay_ref[pl.ds(base + second, third - second)]
    ext = pay_ref[pl.ds(base + tail, rows_all - tail)]
    _, wide = iotas(channels, 2 * channels)
    row, lane = iotas(rows_all - tail, 2 * channels)
    lane = lane - channels
    b_pick = ((row == 2) & ((lane == 0) | (lane == 1))) | (
        (row == 3) & ((lane == 2) | (lane == 3))
    )
    p_pick = (row == 2) & ((lane == 4) | (lane == 5))
    ones = jnp.ones(row.shape, F32)
    folded = folded.astype(F32)
    ext = ext.astype(F32)
    b_side = jnp.transpose(ext)
    columns = dot(b_side[0:channels].astype(BF16), jnp.where(b_pick, ones, 0.0).astype(BF16))
    p_columns = dot(
        b_side[channels : 2 * channels].astype(BF16), jnp.where(p_pick, ones, 0.0).astype(BF16)
    )
    square = jnp.concatenate([folded, pltpu.roll(folded, channels, 1)], axis=0)
    at = pl.ds(h * channels, channels)
    t2[at] = jnp.where(wide < channels, square, columns).astype(BF16)
    t2z[at] = p_columns.astype(BF16)
    a1[pl.ds(h, 1)] = ext[0:1]
    a2[pl.ds(h, 1)] = ext[1:2]
    lows = ext[4 : 4 + tokens // 2]
    pieces = ext[4 + tokens // 2 :]
    low = jnp.concatenate([lows, pltpu.roll(lows, channels, 1)], axis=0)
    whole = (pieces + pltpu.roll(pieces, channels, 1)) + low
    start[pl.ds(h * tokens, tokens)] = whole


def side_kernel(
    times_ref,
    counts_ref,
    w_in_ref,
    wf_ref,
    gain_ref,
    pay_ref,
    out_ref,
    plan_ref,
    t2,
    t2z,
    a1,
    a2,
    start,
    *,
    heads,
    rows_all,
    tokens,
):
    channels, width = w_in_ref.shape
    w_in = w_in_ref[...]
    gram = dot(w_in, w_in, NT) * (1.0 / width)
    gained = w_in.astype(F32) * gain_ref[...].reshape(1, width)
    skip = dot_fine(wf_ref[...], gained)
    for h in range(heads):
        unpack(pay_ref, h * rows_all, h, t2, t2z, a1, a2, start, channels, tokens)
    g_high, g_mid, g_low = split3(gram)
    s_high, s_low = split2(skip)
    out_ref[...] = jnp.concatenate([g_high, g_mid, g_low, s_high, s_low], axis=0)

    lanes = plan_ref.shape[1]
    points = times_ref.shape[1]

    def level(slab_id, column):
        whole = jnp.zeros((1, lanes), jnp.int32) + times_ref[slab_id, column]
        return whole.astype(F32) / 1000.0

    for k in range(2):
        levels = [level(k, column) for column in range(points)]
        last = jnp.zeros((1, lanes), F32)
        for column in range(points):
            last = jnp.where(column == counts_ref[k], levels[column], last)
        steps = [
            jnp.where(j < counts_ref[k], levels[j + 1] - levels[j], 0.0)
            for j in range(points - 1)
        ]
        rows = levels + steps + [last - levels[0]]
        for i, value in enumerate(rows):
            plan_ref[pl.ds(k * 2 * points + i, 1)] = value


def solve_kernel(
    pay_ref,
    side_ref,
    plan_ref,
    t2h_ref,
    t2zh_ref,
    a1h_ref,
    a2h_ref,
    starth_ref,
    before_ref,
    out_ref,
    t2,
    t2z,
    a1,
    a2,
    start,
    *,
    heads,
    tokens,
    slab_id,
    ready,
    points,
):
    slab = lax.axis_index("slab")
    channels = side_ref.shape[1]
    count = heads * tokens
    lanes = 2 * count
    second, third, tail, rows_all = layout(channels, tokens)
    fine_most = points - 1

    @pl.when(slab != slab_id)
    def _():
        out_ref[...] = before_ref[...]

    @pl.when(slab == slab_id)
    def _():
        for h in range(ready, heads):
            unpack(pay_ref, h * rows_all, h, t2, t2z, a1, a2, start, channels, tokens)
        if ready:
            for dst, src in (
                (a1, a1h_ref),
                (a2, a2h_ref),
                (start, starth_ref),
            ):
                dst[0 : src.shape[0]] = src[...]

        def from_half(h, dst, src):
            at = slice(h * channels, (h + 1) * channels)
            return src[at] if h < ready else dst[at]

        _, lane = iotas(1, lanes)
        left = lane < count

        def level(k, column):
            return plan_ref[k * 2 * points + column : k * 2 * points + column + 1]

        def step(k, j):
            return level(k, points + j)

        def span(k):
            return level(k, 2 * points - 1)

        def velocity(u, s):
            rounded = u.astype(BF16)
            sides = dot(side_ref[...], rounded)
            form = (
                sides[0:channels] + sides[channels : 2 * channels]
            ) + sides[2 * channels : 3 * channels]
            squares = jnp.sum(form * rounded.astype(F32), axis=0, keepdims=True)
            r = lax.rsqrt(jnp.maximum(squares, 0.0) + 1e-06)
            skip = r * (sides[3 * channels : 4 * channels] + sides[4 * channels : 5 * channels])
            s2 = s * s
            s_high, s_low = (part.astype(F32) for part in split2(s))
            s2_high, s2_low = (part.astype(F32) for part in split2(s2))
            row, _ = iotas(channels, lanes)
            s_rows = jnp.zeros((channels, lanes), F32)
            for i, value in enumerate((s_high, s_low, s2_high, s2_low, s_high, s_low)):
                s_rows = jnp.where(row == i, value, s_rows)
            x = r * rounded.astype(F32)
            features = jnp.concatenate(
                [x.astype(BF16), (s * x).astype(BF16), (s2 * x).astype(BF16), s_rows.astype(BF16)],
                axis=0,
            )
            keys = jnp.transpose(x)
            keys = jnp.concatenate([keys[0:count], keys[count:lanes]], axis=1).astype(BF16)
            maps = []
            for h in range(heads):
                base = h * rows_all
                maps.append(
                    jnp.concatenate(
                        [pay_ref[base : base + channels], from_half(h, t2, t2h_ref)], axis=1
                    )
                )
            queries = dot(jnp.concatenate(maps, axis=0), features)
            offsets = dot(
                jnp.concatenate([a1[...], a2[...]], axis=1).astype(BF16), features
            )
            maps = []
            for h in range(heads):
                base = h * rows_all
                maps.append(
                    jnp.concatenate(
                        [pay_ref[base + third : base + tail], from_half(h, t2z, t2zh_ref)], axis=1
                    )
                )
            values = dot(jnp.concatenate(maps, axis=0), features).astype(BF16)
            lhs, rhs = [], []
            for h in range(heads):
                at = slice(h * channels, (h + 1) * channels)
                query = queries[at]
                both = jnp.concatenate(
                    [jnp.where(left, query, 0.0), jnp.where(left, 0.0, query)], axis=0
                )
                scores = dot(keys, both.astype(BF16)) + offsets[h : h + 1]
                raised = jnp.exp2(scores - jnp.max(scores, axis=0, keepdims=True))
                weights = raised / jnp.sum(raised, axis=0, keepdims=True)
                lhs.append(values[at])
                rhs.append(jnp.where(left, weights, 0.0).astype(BF16))
                rhs.append(jnp.where(left, 0.0, weights).astype(BF16))
            return skip + dot(jnp.concatenate(lhs, axis=1), jnp.concatenate(rhs, axis=0))

        noise = jnp.transpose(start[...])[0:channels]
        noise = jnp.concatenate([noise, noise], axis=1)
        moved = velocity(noise, level(0, 0))
        first_coarse = noise + span(0) * moved
        if slab_id == 0:
            u = noise + step(0, 0) * moved
            for j in range(1, fine_most):
                u = u + step(0, j) * velocity(u, level(0, j))
            ended = first_coarse + (u - first_coarse)
        else:
            u = jnp.where(left, noise + step(0, 0) * moved, first_coarse)
            coarse_old = None
            for j in range(fine_most):
                last = j == fine_most - 1
                s = jnp.where(left, level(1, 0) if last else level(0, j + 1), level(1, j))
                moved = velocity(u, s)
                if j == 0:
                    coarse_old = u + span(1) * moved
                u = u + jnp.where(left, span(1) if last else step(0, j + 1), step(1, j)) * moved
            ended = u + pltpu.roll(u - coarse_old, count, 1)
        out_ref[...] = jnp.transpose(ended)[0:tokens, 0:channels]


def exchanged(value, stride):
    groups, size, slabs = (lax.axis_size(axis) for axis in ("groups", "seq", "slab"))
    pairs = []
    for g in range(groups):
        for s in range(size):
            for c in range(slabs):
                if c == slabs - 1 or groups % 2:
                    to = (g, s ^ stride)
                else:
                    to = (g ^ 1, s)
                pairs.append(((g * size + s) * slabs + c, (to[0] * size + to[1]) * slabs + c))
    return lax.ppermute(value, ("groups", "seq", "slab"), pairs)


def local(
    noise,
    timesteps,
    fine_counts,
    w_in,
    w_query,
    w_key,
    w_value,
    w_out,
    w_final,
    mod_scale,
    mod_shift,
    skip_gain,
):
    channels, width = w_in.shape
    tokens = noise.shape[0]
    heads = lax.axis_size("seq")
    half = heads // 2
    count = tokens * heads
    points = timesteps.shape[1]
    *_, rows = layout(channels, tokens)
    wf_t = w_final.T
    vmem = pl.BlockSpec(memory_space=pltpu.VMEM)
    smem = pl.BlockSpec(memory_space=pltpu.SMEM)
    hbm = pl.BlockSpec(memory_space=pl.ANY)
    chunks = 5

    def near(*values):
        return [pltpu.with_memory_space_constraint(value, pltpu.VMEM) for value in values]

    packed = pl.pallas_call(
        functools.partial(fold_kernel, chunks=chunks),
        out_shape=pltpu.VMEM((rows, 2 * channels), BF16),
        in_specs=[vmem, hbm, hbm, hbm, hbm, hbm, hbm, vmem, vmem],
        out_specs=vmem,
        scratch_shapes=[
            pltpu.VMEM((channels, width), BF16),
            pltpu.VMEM((3 * channels + 16, width), BF16),
            pltpu.VMEM((width, HEAD_SIZE), BF16),
            pltpu.VMEM((width, HEAD_SIZE), BF16),
            pltpu.VMEM((width, HEAD_SIZE), BF16),
            pltpu.VMEM((HEAD_SIZE, width), BF16),
            pltpu.VMEM((channels, width), F32),
            pltpu.VMEM((2 * channels, width), BF16),
            pltpu.SemaphoreType.DMA((3 * chunks + 3,)),
        ],
        name="fold",
    )(noise, w_in, w_query, w_key, w_value, w_out, wf_t, mod_scale, mod_shift)
    stride = half
    own = packed
    while stride > 1:
        own = jnp.concatenate([own, exchanged(own, stride)], axis=0)
        stride //= 2

    def tables(n, kind):
        return (
            kind((n * channels, 2 * channels), BF16),
            kind((n * channels, 2 * channels), BF16),
            kind((n, 2 * channels), F32),
            kind((n, 2 * channels), F32),
            kind((n * tokens, 2 * channels), F32),
        )

    side, plan, *firsts = pl.pallas_call(
        functools.partial(side_kernel, heads=half, rows_all=rows, tokens=tokens),
        out_shape=(
            pltpu.VMEM((5 * channels, channels), BF16),
            pltpu.VMEM((4 * points, 2 * count), F32),
            *tables(half, pltpu.VMEM),
        ),
        in_specs=[smem, smem, vmem, vmem, vmem, vmem],
        out_specs=(vmem,) * 7,
        name="side",
    )(timesteps, fine_counts, w_in, wf_t, skip_gain, *near(own))
    own = jnp.concatenate([own, exchanged(own, 1)], axis=0)
    own, side, plan, *firsts = lax.optimization_barrier((own, side, plan, *firsts))
    other = lax.ppermute(own, "slab", [(0, 1), (1, 0)])

    def solve(slab_id, pay, before, kind):
        return pl.pallas_call(
            functools.partial(
                solve_kernel,
                heads=heads,
                tokens=tokens,
                slab_id=slab_id,
                ready=half if slab_id else 0,
                points=points,
            ),
            out_shape=kind((tokens, channels), F32),
            in_specs=[vmem] * 9,
            out_specs=vmem,
            scratch_shapes=tables(heads, pltpu.VMEM),
            name=f"solve{slab_id}",
        )(*near(pay, side, plan, *firsts, before))

    ended = solve(1, own, plan[0:tokens, 0:channels], pltpu.VMEM)
    ended = solve(0, other, ended, jax.ShapeDtypeStruct)
    return ended[None]


def solution(mesh):
    placed = (
        P(("groups", "seq"), None),
        P("groups", None),
        P("groups"),
        P(),
        P(None, "seq"),
        P(None, "seq"),
        P(None, "seq"),
        P("seq", None),
        P(),
        P(),
        P(),
        P(),
    )
    return jax.shard_map(
        local,
        mesh=mesh,
        in_specs=placed,
        out_specs=P("slab", ("groups", "seq"), None),
        check_vma=False,
    )
```

```python
import functools
import math

import jax
import jax.numpy as jnp
from jax import lax
from jax.experimental import pallas as pl
from jax.experimental.pallas import tpu as pltpu
from jax.sharding import PartitionSpec as P

HEAD_SIZE = 128
F32 = jnp.float32
BF16 = jnp.bfloat16
NT = (((1,), (1,)), ((), ()))
TN = (((0,), (0,)), ((), ()))


def dot(a, b, dims=(((1,), (0,)), ((), ()))):
    return lax.dot_general(a, b, dims, preferred_element_type=F32)


def split2(x):
    high = x.astype(BF16)
    return high, (x - high.astype(F32)).astype(BF16)


def split3(x):
    high = x.astype(BF16)
    mid, low = split2(x - high.astype(F32))
    return high, mid, low


def dot_fine(a, b):
    a_high, a_low = split2(a)
    b_high, b_low = split2(b)
    return dot(
        jnp.concatenate([a_high, a_high, a_low], axis=1),
        jnp.concatenate([b_high, b_low, b_high], axis=1),
        NT,
    )


def layout(channels, tokens):
    second = channels
    third = second + channels // 2
    tail = third + channels
    return second, third, tail, tail + 4 + tokens // 2 + tokens


def iotas(rows, columns):
    return (
        lax.broadcasted_iota(jnp.int32, (rows, columns), 0),
        lax.broadcasted_iota(jnp.int32, (rows, columns), 1),
    )


def fold_kernel(
    noise_hbm,
    w_in_hbm,
    wq_hbm,
    wk_hbm,
    wv_hbm,
    wo_hbm,
    wf_hbm,
    scale_hbm,
    shift_hbm,
    out_ref,
    noise,
    w_in,
    lift,
    w_a,
    w_b,
    w_c,
    wo,
    wf,
    wf2,
    scale,
    shift,
    sems,
):
    slab = lax.axis_index("slab")
    channels, width = w_in.shape
    half = channels // 2
    tokens = noise.shape[0]
    second, third, tail, rows_all = layout(channels, tokens)

    def parts(total):
        last = total[3 * channels : 3 * channels + 8]
        return (
            total[0:channels],
            total[channels : 2 * channels] + total[2 * channels : 3 * channels],
            last[0:1] + last[1:2],
        )

    @pl.when(slab == 0)
    def _():
        out_ref[...] = jnp.zeros_like(out_ref)

    @pl.when(slab != 0)
    def _():
        moves = (
            (w_in_hbm, w_in),
            (scale_hbm, scale),
            (shift_hbm, shift),
            (wf_hbm, wf),
            (wq_hbm, w_a),
            (wk_hbm, w_b),
            (wv_hbm, w_c),
            (wo_hbm, wo),
            (noise_hbm, noise),
        )
        copies = []
        for i, (src, dst) in enumerate(moves):
            copies.append(pltpu.make_async_copy(src, dst, sems.at[i]))
            copies[-1].start()
        for copy in copies[:3]:
            copy.wait()
        lift[0:channels] = w_in[...]
        high, low = split2(w_in[...].astype(F32) * scale[...].reshape(1, width))
        lift[channels : 2 * channels] = high
        lift[2 * channels : 3 * channels] = low
        shift_high, shift_low = split2(shift[...].reshape(1, width))
        row, _ = iotas(16, width)
        lift[3 * channels : 3 * channels + 16] = jnp.where(
            row == 0,
            shift_high.astype(F32),
            jnp.where(row == 1, shift_low.astype(F32), 0.0),
        ).astype(BF16)
        copies[3].wait()
        high, low = split2(wf[...])
        wf2[0:channels] = high
        wf2[channels : 2 * channels] = low
        for copy in copies[4:]:
            copy.wait()
        total = dot(lift[...], jnp.concatenate([w_a[...], w_b[...], w_c[...]], axis=1))
        both = dot(wf2[...], wo[...], NT)
        out_t = both[0:channels] + both[channels : 2 * channels]
        q0, q1, q2 = parts(total[:, 0:HEAD_SIZE] * (math.log2(math.e) / math.sqrt(HEAD_SIZE)))
        k0, k1, k2 = parts(total[:, HEAD_SIZE : 2 * HEAD_SIZE])
        v0, v1, v2 = parts(total[:, 2 * HEAD_SIZE : 3 * HEAD_SIZE])
        pad = jnp.zeros((7, HEAD_SIZE), F32)
        q_all = jnp.concatenate([q0, q1], axis=0)
        k_all = jnp.concatenate([k0, k1], axis=0)
        form = dot_fine(k_all, q_all)
        a_rows = dot_fine(jnp.concatenate([k2, pad], axis=0), q_all)
        b_rows = dot_fine(jnp.concatenate([q2, pad], axis=0), k_all)
        constant = jnp.sum(k2 * q2)
        p_rows = dot_fine(
            jnp.concatenate([v2, pad], axis=0), jnp.concatenate([out_t, out_t], axis=0)
        )
        _, lane = iotas(channels, 2 * channels)
        top, bottom = form[0:channels], form[channels : 2 * channels]
        rolled = pltpu.roll(bottom, channels, 1)
        out_ref[0:channels] = jnp.where(lane < channels, top, top + rolled).astype(BF16)
        out_ref[second:third] = jnp.where(
            lane[0:half] < channels, rolled[0:half], bottom[half:channels]
        ).astype(BF16)
        out_ref[third:tail] = dot_fine(out_t, jnp.concatenate([v0, v1], axis=0)).astype(BF16)
        n_high, n_mid, n_low = (part.astype(F32) for part in split3(noise[...]))
        lows = jnp.concatenate([n_low[0 : tokens // 2], n_low[tokens // 2 : tokens]], axis=1)
        row, lane = iotas(4, 2 * channels)
        left = lane < channels
        a_roll = pltpu.roll(a_rows, channels, 1)[0:1]
        b_roll = pltpu.roll(b_rows, channels, 1)[0:1]
        vectors = jnp.where(
            row == 0,
            jnp.where(left, 0.0, a_roll),
            jnp.where(
                row == 1,
                jnp.where(left, a_roll, constant),
                jnp.where(
                    row == 2,
                    jnp.where(left, 0.0, b_roll),
                    jnp.where(left, b_roll, p_rows[0:1]),
                ),
            ),
        )
        out_ref[tail:rows_all] = jnp.concatenate(
            [vectors, lows, jnp.concatenate([n_high, n_mid], axis=1)], axis=0
        ).astype(BF16)


def unpack(pay_ref, base, h, tables, channels, tokens):
    squares, *vectors, start = tables
    second, third, tail, rows_all = layout(channels, tokens)
    folded = pay_ref[pl.ds(base + second, third - second)].astype(F32)
    ext = pay_ref[pl.ds(base + tail, rows_all - tail)].astype(F32)
    at = pl.ds(h * channels, channels)
    squares[at] = jnp.concatenate([folded, pltpu.roll(folded, channels, 1)], axis=0).astype(BF16)
    for i, vector in enumerate(vectors):
        vector[pl.ds(h, 1)] = ext[i : i + 1]
    lows = ext[4 : 4 + tokens // 2]
    pieces = ext[4 + tokens // 2 :]
    low = jnp.concatenate([lows, pltpu.roll(lows, channels, 1)], axis=0)
    start[pl.ds(h * tokens, tokens)] = (pieces + pltpu.roll(pieces, channels, 1)) + low


def side_kernel(
    times_ref,
    counts_ref,
    w_in_ref,
    wf_ref,
    gain_ref,
    pay_ref,
    out_ref,
    plan_ref,
    *tables,
    heads,
    rows_all,
    tokens,
):
    channels, width = w_in_ref.shape
    w_in = w_in_ref[...]
    gram = dot(w_in, w_in, NT) * (1.0 / width)
    gained = w_in.astype(F32) * gain_ref[...].reshape(1, width)
    skip = dot_fine(wf_ref[...], gained)
    for h in range(heads):
        unpack(pay_ref, h * rows_all, h, tables, channels, tokens)
    g_high, g_mid, g_low = split3(gram)
    s_high, s_low = split2(skip)
    zero = jnp.zeros_like(s_high)
    out_ref[...] = jnp.concatenate(
        [
            jnp.concatenate([g_high, g_mid], axis=1),
            jnp.concatenate([s_high, s_low], axis=1),
            jnp.concatenate([g_low, zero], axis=1),
            jnp.concatenate([zero, zero], axis=1),
        ],
        axis=0,
    )

    lanes = plan_ref.shape[1]
    points = times_ref.shape[1]

    def level(slab_id, column):
        whole = jnp.zeros((1, lanes), jnp.int32) + times_ref[slab_id, column]
        return whole.astype(F32) / 1000.0

    for k in range(2):
        levels = [level(k, column) for column in range(points)]
        last = jnp.zeros((1, lanes), F32)
        for column in range(points):
            last = jnp.where(column == counts_ref[k], levels[column], last)
        steps = [
            jnp.where(j < counts_ref[k], levels[j + 1] - levels[j], 0.0)
            for j in range(points - 1)
        ]
        rows = levels + steps + [last - levels[0]]
        for i, value in enumerate(rows):
            plan_ref[pl.ds(k * 2 * points + i, 1)] = value


def solve_kernel(
    pay_ref,
    side_ref,
    plan_ref,
    *refs,
    heads,
    tokens,
    slab_id,
    ready,
    points,
):
    firsts, before_ref, out_ref, tables = refs[:6], refs[6], refs[7], refs[8:]
    squares, a_first, a_second, b_first, b_second, start = tables
    slab = lax.axis_index("slab")
    channels = side_ref.shape[1] // 2
    count = heads * tokens
    blocks = 1 + slab_id
    lanes = blocks * count
    second, third, tail, rows_all = layout(channels, tokens)
    fine_most = points - 1

    @pl.when(slab != slab_id)
    def _():
        out_ref[...] = before_ref[...]

    @pl.when(slab == slab_id)
    def _():
        for h in range(ready, heads):
            unpack(pay_ref, h * rows_all, h, tables, channels, tokens)
        if ready:
            for table, first in zip(tables[1:], firsts[1:]):
                table[0 : first.shape[0]] = first[...]

        def square(h):
            at = slice(h * channels, (h + 1) * channels)
            return firsts[0][at] if h < ready else squares[at]

        _, lane = iotas(1, lanes)
        left = lane < count
        constants = jnp.broadcast_to(a_second[:, channels : channels + 1], (heads, lanes))
        vector_maps = jnp.concatenate(
            [
                jnp.concatenate([b_first[...], a_first[...]], axis=0),
                jnp.concatenate([b_second[...], a_second[...]], axis=0),
            ],
            axis=1,
        ).astype(BF16)
        p_row = jnp.sum(b_second[...], axis=0, keepdims=True)
        p_row = jnp.broadcast_to(p_row, (8, 2 * channels))
        p_sum = jnp.broadcast_to(
            jnp.transpose(p_row)[channels : 2 * channels, 0:1], (channels, lanes)
        )
        row, column = iotas(blocks * heads, lanes)
        selectors = []
        for h in range(heads):
            if blocks == 1:
                mine = row == h
            else:
                mine = ((row == h) & (column >= count)) | ((row == heads + h) & (column < count))
            selectors.append(jnp.where(mine, 1.0, 0.0).astype(BF16))

        def level(k, column):
            row = k * 2 * points + column
            return plan_ref[row : row + 1, 0:lanes]

        def step(k, j):
            return level(k, points + j)

        def span(k):
            return level(k, 2 * points - 1)

        def by_block(row):
            if blocks == 1:
                return [row]
            return [jnp.where(left, row, 0.0), jnp.where(left, 0.0, row)]

        def key_side(rows):
            turned = jnp.transpose(rows)
            if blocks == 1:
                return turned[:, 0 : channels + heads].astype(BF16)
            first, last = turned[0:count], turned[count:lanes]
            rolled = pltpu.roll(last, channels, 1)
            terms = pltpu.roll(first, channels + heads, 1)
            _, lane = iotas(count, 2 * channels)
            one = jnp.where(lane < channels, first, rolled)
            two = jnp.where(lane < heads, rolled, terms)
            return jnp.concatenate([one, two[:, 0 : 2 * heads]], axis=1).astype(BF16)

        def velocity(u, s):
            rounded = u.astype(BF16)
            wide = rounded.astype(F32)
            s2 = s * s
            features = jnp.concatenate(
                [
                    rounded,
                    (s * wide).astype(BF16),
                    (s2 * wide).astype(BF16),
                    jnp.zeros((channels, lanes), BF16),
                ],
                axis=0,
            )
            twice = jnp.concatenate([rounded, rounded], axis=0)
            sides = dot(side_ref[0 : 2 * channels], twice) + dot(
                side_ref[2 * channels : 4 * channels], twice
            )
            norm = jnp.sum(sides[0:channels] * wide, axis=0, keepdims=True)
            r = lax.rsqrt(jnp.maximum(norm, 0.0) + 1e-06)
            maps = [vector_maps]
            for h in range(heads):
                base = h * rows_all
                maps.append(jnp.concatenate([pay_ref[base : base + channels], square(h)], axis=1))
            product = dot(jnp.concatenate(maps, axis=0), features)
            values = dot(
                jnp.concatenate(
                    [
                        pay_ref[h * rows_all + third : h * rows_all + tail]
                        for h in range(heads)
                    ],
                    axis=0,
                ),
                features[0 : 2 * channels],
            )
            offsets = r * product[heads : 2 * heads] + s2 * constants
            blank = jnp.zeros((channels - heads, lanes), F32)
            keys = key_side(jnp.concatenate([r * wide, r * product[0:heads], blank], axis=0))
            r_blocks = by_block(r)
            at_queries = 2 * heads
            rhs, pairs = [], []
            for h in range(heads):
                at = at_queries + h * channels
                raw = product[at : at + channels]
                query = [(raw * part).astype(BF16) for part in r_blocks]
                pairs.append(jnp.concatenate([*query, selectors[h]], axis=0))
            if blocks == 1:
                all_scores = [dot(keys, pair) for pair in pairs]
            else:
                joined = dot(keys, jnp.concatenate(pairs, axis=1))
                all_scores = [
                    joined[:, h * lanes : (h + 1) * lanes] for h in range(heads)
                ]
            for h in range(heads):
                scores = all_scores[h] + offsets[h : h + 1]
                raised = jnp.exp2(scores - jnp.max(scores, axis=0, keepdims=True))
                inverse = 1.0 / jnp.sum(raised, axis=0, keepdims=True)
                rhs += [(raised * part).astype(BF16) for part in by_block(inverse)]
            values = [
                (r * values[h * channels : (h + 1) * channels]).astype(BF16)
                for h in range(heads)
            ]
            mixed = dot(jnp.concatenate(values, axis=1), jnp.concatenate(rhs, axis=0))
            return (r * sides[channels : 2 * channels] + s * p_sum) + mixed

        noise = jnp.transpose(start[...])[0:channels]
        noise = jnp.concatenate([noise] * blocks, axis=1)
        moved = velocity(noise, level(0, 0))
        first_coarse = noise + span(0) * moved
        if slab_id == 0:
            u = noise + step(0, 0) * moved
            for j in range(1, fine_most):
                u = u + step(0, j) * velocity(u, level(0, j))
            ended = first_coarse + (u - first_coarse)
        else:
            u = jnp.where(left, noise + step(0, 0) * moved, first_coarse)
            coarse_old = None
            for j in range(fine_most):
                last = j == fine_most - 1
                s = jnp.where(left, level(1, 0) if last else level(0, j + 1), level(1, j))
                moved = velocity(u, s)
                if j == 0:
                    coarse_old = u + span(1) * moved
                u = u + jnp.where(left, span(1) if last else step(0, j + 1), step(1, j)) * moved
            ended = u + pltpu.roll(u - coarse_old, count, 1)
        out_ref[...] = jnp.transpose(ended)[0:tokens, 0:channels]


def exchanged(value, stride):
    groups, size, slabs = (lax.axis_size(axis) for axis in ("groups", "seq", "slab"))
    pairs = []
    for g in range(groups):
        for s in range(size):
            for c in range(slabs):
                if c == slabs - 1 or groups % 2:
                    to = (g, s ^ stride)
                else:
                    to = (g ^ 1, s)
                pairs.append(((g * size + s) * slabs + c, (to[0] * size + to[1]) * slabs + c))
    return lax.ppermute(value, ("groups", "seq", "slab"), pairs)


def local(
    noise,
    timesteps,
    fine_counts,
    w_in,
    w_query,
    w_key,
    w_value,
    w_out,
    w_final,
    mod_scale,
    mod_shift,
    skip_gain,
):
    channels, width = w_in.shape
    tokens = noise.shape[0]
    heads = lax.axis_size("seq")
    half = heads // 2
    count = tokens * heads
    points = timesteps.shape[1]
    *_, rows = layout(channels, tokens)
    wf_t = w_final.T
    vmem = pl.BlockSpec(memory_space=pltpu.VMEM)
    smem = pl.BlockSpec(memory_space=pltpu.SMEM)
    hbm = pl.BlockSpec(memory_space=pl.ANY)

    def near(*values):
        return [pltpu.with_memory_space_constraint(value, pltpu.VMEM) for value in values]

    packed = pl.pallas_call(
        fold_kernel,
        out_shape=pltpu.VMEM((rows, 2 * channels), BF16),
        in_specs=[hbm] * 9,
        out_specs=vmem,
        scratch_shapes=[
            pltpu.VMEM((tokens, channels), F32),
            pltpu.VMEM((channels, width), BF16),
            pltpu.VMEM((3 * channels + 16, width), BF16),
            pltpu.VMEM((width, HEAD_SIZE), BF16),
            pltpu.VMEM((width, HEAD_SIZE), BF16),
            pltpu.VMEM((width, HEAD_SIZE), BF16),
            pltpu.VMEM((HEAD_SIZE, width), BF16),
            pltpu.VMEM((channels, width), F32),
            pltpu.VMEM((2 * channels, width), BF16),
            pltpu.VMEM((width,), F32),
            pltpu.VMEM((width,), F32),
            pltpu.SemaphoreType.DMA((9,)),
        ],
        name="fold",
    )(noise, w_in, w_query, w_key, w_value, w_out, wf_t, mod_scale, mod_shift)
    stride = half
    own = packed
    while stride > 1:
        own = jnp.concatenate([own, exchanged(own, stride)], axis=0)
        stride //= 2

    def tables(n, kind):
        return (
            kind((n * channels, 2 * channels), BF16),
            *(kind((n, 2 * channels), F32) for _ in range(4)),
            kind((n * tokens, 2 * channels), F32),
        )

    side, plan, *firsts = pl.pallas_call(
        functools.partial(side_kernel, heads=half, rows_all=rows, tokens=tokens),
        out_shape=(
            pltpu.VMEM((4 * channels, 2 * channels), BF16),
            pltpu.VMEM((4 * points, 2 * count), F32),
            *tables(half, pltpu.VMEM),
        ),
        in_specs=[smem, smem, vmem, vmem, vmem, vmem],
        out_specs=(vmem,) * 8,
        name="side",
    )(timesteps, fine_counts, w_in, wf_t, skip_gain, *near(own))
    own = jnp.concatenate([own, exchanged(own, 1)], axis=0)
    own, side, plan, *firsts = lax.optimization_barrier((own, side, plan, *firsts))
    other = lax.ppermute(own, "slab", [(0, 1), (1, 0)])

    def solve(slab_id, pay, before, kind):
        return pl.pallas_call(
            functools.partial(
                solve_kernel,
                heads=heads,
                tokens=tokens,
                slab_id=slab_id,
                ready=half if slab_id else 0,
                points=points,
            ),
            out_shape=kind((tokens, channels), F32),
            in_specs=[vmem] * 10,
            out_specs=vmem,
            scratch_shapes=tables(heads, pltpu.VMEM),
            name=f"solve{slab_id}",
        )(*near(pay, side, plan, *firsts, before))

    ended = solve(1, own, plan[0:tokens, 0:channels], pltpu.VMEM)
    ended = solve(0, other, ended, jax.ShapeDtypeStruct)
    return ended[None]


def solution(mesh):
    placed = (
        P(("groups", "seq"), None),
        P("groups", None),
        P("groups"),
        P(),
        P(None, "seq"),
        P(None, "seq"),
        P(None, "seq"),
        P("seq", None),
        P(),
        P(),
        P(),
        P(),
    )
    return jax.shard_map(
        local,
        mesh=mesh,
        in_specs=placed,
        out_specs=P("slab", ("groups", "seq"), None),
        check_vma=False,
    )
```

```python
import functools
import math

import jax
import jax.numpy as jnp
from jax import lax
from jax.experimental import pallas as pl
from jax.experimental.pallas import tpu as pltpu
from jax.sharding import PartitionSpec as P

HEAD_SIZE = 128
F32 = jnp.float32
BF16 = jnp.bfloat16
NT = (((1,), (1,)), ((), ()))
TN = (((0,), (0,)), ((), ()))


def dot(a, b, dims=(((1,), (0,)), ((), ()))):
    return lax.dot_general(a, b, dims, preferred_element_type=F32)


def split2(x):
    high = x.astype(BF16)
    return high, (x - high.astype(F32)).astype(BF16)


def split3(x):
    high = x.astype(BF16)
    mid, low = split2(x - high.astype(F32))
    return high, mid, low


def dot_fine(a, b):
    a_high, a_low = split2(a)
    b_high, b_low = split2(b)
    return dot(
        jnp.concatenate([a_high, a_high, a_low], axis=1),
        jnp.concatenate([b_high, b_low, b_high], axis=1),
        NT,
    )


def layout(channels, tokens):
    second = channels
    third = second + channels // 2
    tail = third + channels
    return second, third, tail, tail + 4 + tokens // 2 + tokens


def iotas(rows, columns):
    return (
        lax.broadcasted_iota(jnp.int32, (rows, columns), 0),
        lax.broadcasted_iota(jnp.int32, (rows, columns), 1),
    )


def fold_kernel(
    noise_hbm,
    w_in_hbm,
    wq_hbm,
    wk_hbm,
    wv_hbm,
    wo_hbm,
    wf_hbm,
    scale_hbm,
    shift_hbm,
    out_ref,
    noise,
    w_in,
    w_a,
    w_b,
    w_c,
    wo,
    wf,
    scale,
    shift,
    sems,
    *,
    pieces,
):
    slab = lax.axis_index("slab")
    channels, width = w_in.shape
    half = channels // 2
    tokens = noise.shape[0]
    second, third, tail, rows_all = layout(channels, tokens)

    def parts(total):
        last = total[2 * channels : 2 * channels + 8]
        return total[0:channels], total[channels : 2 * channels], last[0:1] + last[1:2]

    @pl.when(slab == 0)
    def _():
        out_ref[...] = jnp.zeros_like(out_ref)

    @pl.when(slab != 0)
    def _():
        used = 0

        def fetch(src, dst):
            nonlocal used
            copy = pltpu.make_async_copy(src, dst, sems.at[used])
            copy.start()
            used += 1
            return copy

        waits = [fetch(w_in_hbm, w_in), fetch(scale_hbm, scale), fetch(shift_hbm, shift)]
        tiles = width // HEAD_SIZE
        cuts = [tiles * k // pieces // 2 * 2 * HEAD_SIZE for k in range(pieces)] + [width]
        pulls = []
        for low, high in zip(cuts, cuts[1:]):
            at = pl.ds(low, high - low)
            pulls.append(
                [
                    fetch(src.at[at], dst.at[at])
                    for src, dst in ((wq_hbm, w_a), (wk_hbm, w_b), (wv_hbm, w_c))
                ]
            )
        finals = [fetch(wf_hbm, wf), fetch(wo_hbm, wo), fetch(noise_hbm, noise)]
        total = None
        for copy in waits:
            copy.wait()
        factors = scale[...].reshape(1, width)
        shift_high, shift_low = split2(shift[...].reshape(1, width))
        shift_high, shift_low = shift_high.astype(F32), shift_low.astype(F32)
        for low, high, pull in zip(cuts, cuts[1:], pulls):
            for copy in pull:
                copy.wait()
            at = slice(low, high)
            plain = w_in[:, at]
            scaled = plain.astype(F32) * factors[:, at]
            row, _ = iotas(16, high - low)
            vectors = jnp.where(
                row == 0, shift_high[:, at], jnp.where(row == 1, shift_low[:, at], 0.0)
            )
            lift = jnp.concatenate([plain, scaled.astype(BF16), vectors.astype(BF16)], axis=0)
            term = dot(lift, jnp.concatenate([w_a[at], w_b[at], w_c[at]], axis=1))
            total = term if total is None else total + term
        for copy in finals:
            copy.wait()
        both = dot(jnp.concatenate(split2(wf[...]), axis=0), wo[...], NT)
        out_t = both[0:channels] + both[channels : 2 * channels]
        q0, q1, q2 = parts(total[:, 0:HEAD_SIZE] * (math.log2(math.e) / math.sqrt(HEAD_SIZE)))
        k0, k1, k2 = parts(total[:, HEAD_SIZE : 2 * HEAD_SIZE])
        v0, v1, v2 = parts(total[:, 2 * HEAD_SIZE : 3 * HEAD_SIZE])
        pad = jnp.zeros((7, HEAD_SIZE), F32)
        q_all = jnp.concatenate([q0, q1], axis=0)
        k_all = jnp.concatenate([k0, k1], axis=0)
        form = dot_fine(k_all, q_all)
        a_rows = dot_fine(jnp.concatenate([k2, pad], axis=0), q_all)
        b_rows = dot_fine(jnp.concatenate([q2, pad], axis=0), k_all)
        constant = jnp.sum(k2 * q2)
        p_rows = dot_fine(
            jnp.concatenate([v2, pad], axis=0), jnp.concatenate([out_t, out_t], axis=0)
        )
        _, lane = iotas(channels, 2 * channels)
        top, bottom = form[0:channels], form[channels : 2 * channels]
        rolled = pltpu.roll(bottom, channels, 1)
        out_ref[0:channels] = jnp.where(lane < channels, top, top + rolled).astype(BF16)
        out_ref[second:third] = jnp.where(
            lane[0:half] < channels, rolled[0:half], bottom[half:channels]
        ).astype(BF16)
        out_ref[third:tail] = dot_fine(out_t, jnp.concatenate([v0, v1], axis=0)).astype(BF16)
        n_high, n_mid, n_low = (part.astype(F32) for part in split3(noise[...]))
        lows = jnp.concatenate([n_low[0 : tokens // 2], n_low[tokens // 2 : tokens]], axis=1)
        row, lane = iotas(4, 2 * channels)
        left = lane < channels
        a_roll = pltpu.roll(a_rows, channels, 1)[0:1]
        b_roll = pltpu.roll(b_rows, channels, 1)[0:1]
        vectors = jnp.where(
            row == 0,
            jnp.where(left, 0.0, a_roll),
            jnp.where(
                row == 1,
                jnp.where(left, a_roll, constant),
                jnp.where(
                    row == 2,
                    jnp.where(left, 0.0, b_roll),
                    jnp.where(left, b_roll, p_rows[0:1]),
                ),
            ),
        )
        out_ref[tail:rows_all] = jnp.concatenate(
            [vectors, lows, jnp.concatenate([n_high, n_mid], axis=1)], axis=0
        ).astype(BF16)


def unpack(pay_ref, base, h, tables, channels, tokens):
    squares, *vectors, start = tables
    second, third, tail, rows_all = layout(channels, tokens)
    folded = pay_ref[pl.ds(base + second, third - second)].astype(F32)
    ext = pay_ref[pl.ds(base + tail, rows_all - tail)].astype(F32)
    at = pl.ds(h * channels, channels)
    squares[at] = jnp.concatenate([folded, pltpu.roll(folded, channels, 1)], axis=0).astype(BF16)
    for i, vector in enumerate(vectors):
        vector[pl.ds(h, 1)] = ext[i : i + 1]
    lows = ext[4 : 4 + tokens // 2]
    pieces = ext[4 + tokens // 2 :]
    low = jnp.concatenate([lows, pltpu.roll(lows, channels, 1)], axis=0)
    start[pl.ds(h * tokens, tokens)] = (pieces + pltpu.roll(pieces, channels, 1)) + low


def side_kernel(
    times_ref,
    counts_ref,
    w_in_ref,
    wf_ref,
    gain_ref,
    pay_ref,
    out_ref,
    plan_ref,
    *tables,
    heads,
    rows_all,
    tokens,
):
    channels, width = w_in_ref.shape
    w_in = w_in_ref[...]
    gram = dot(w_in, w_in, NT) * (1.0 / width)
    gained = w_in.astype(F32) * gain_ref[...].reshape(1, width)
    skip = dot_fine(wf_ref[...], gained)
    for h in range(heads):
        unpack(pay_ref, h * rows_all, h, tables, channels, tokens)
    g_high, g_mid, g_low = split3(gram)
    s_high, s_low = split2(skip)
    zero = jnp.zeros_like(s_high)
    out_ref[...] = jnp.concatenate(
        [
            jnp.concatenate([g_high, g_mid], axis=1),
            jnp.concatenate([s_high, s_low], axis=1),
            jnp.concatenate([g_low, zero], axis=1),
            jnp.concatenate([zero, zero], axis=1),
        ],
        axis=0,
    )

    lanes = plan_ref.shape[1]
    points = times_ref.shape[1]

    def level(slab_id, column):
        whole = jnp.zeros((1, lanes), jnp.int32) + times_ref[slab_id, column]
        return whole.astype(F32) / 1000.0

    for k in range(2):
        levels = [level(k, column) for column in range(points)]
        last = jnp.zeros((1, lanes), F32)
        for column in range(points):
            last = jnp.where(column == counts_ref[k], levels[column], last)
        steps = [
            jnp.where(j < counts_ref[k], levels[j + 1] - levels[j], 0.0)
            for j in range(points - 1)
        ]
        rows = levels + steps + [last - levels[0]]
        for i, value in enumerate(rows):
            plan_ref[pl.ds(k * 2 * points + i, 1)] = value


def solve_kernel(
    pay_ref,
    side_ref,
    plan_ref,
    *refs,
    heads,
    tokens,
    slab_id,
    ready,
    points,
):
    firsts, before_ref, out_ref, tables = refs[:6], refs[6], refs[7], refs[8:]
    squares, a_first, a_second, b_first, b_second, start = tables
    slab = lax.axis_index("slab")
    channels = side_ref.shape[1] // 2
    count = heads * tokens
    blocks = 1 + slab_id
    lanes = blocks * count
    second, third, tail, rows_all = layout(channels, tokens)
    fine_most = points - 1

    @pl.when(slab != slab_id)
    def _():
        out_ref[...] = before_ref[...]

    @pl.when(slab == slab_id)
    def _():
        for h in range(ready, heads):
            unpack(pay_ref, h * rows_all, h, tables, channels, tokens)
        if ready:
            for table, first in zip(tables[1:], firsts[1:]):
                table[0 : first.shape[0]] = first[...]

        def square(h):
            at = slice(h * channels, (h + 1) * channels)
            return firsts[0][at] if h < ready else squares[at]

        _, lane = iotas(1, lanes)
        left = lane < count
        constants = jnp.broadcast_to(a_second[:, channels : channels + 1], (heads, lanes))
        vector_maps = jnp.concatenate(
            [
                jnp.concatenate([b_first[...], a_first[...]], axis=0),
                jnp.concatenate([b_second[...], a_second[...]], axis=0),
            ],
            axis=1,
        ).astype(BF16)
        p_row = jnp.sum(b_second[...], axis=0, keepdims=True)
        p_row = jnp.broadcast_to(p_row, (8, 2 * channels))
        p_sum = jnp.broadcast_to(
            jnp.transpose(p_row)[channels : 2 * channels, 0:1], (channels, lanes)
        )
        row, column = iotas(blocks * heads, lanes)
        selectors = []
        for h in range(heads):
            if blocks == 1:
                mine = row == h
            else:
                mine = ((row == h) & (column >= count)) | ((row == heads + h) & (column < count))
            selectors.append(jnp.where(mine, 1.0, 0.0).astype(BF16))

        def level(k, column):
            row = k * 2 * points + column
            return plan_ref[row : row + 1, 0:lanes]

        def step(k, j):
            return level(k, points + j)

        def span(k):
            return level(k, 2 * points - 1)

        def by_block(row):
            if blocks == 1:
                return [row]
            return [jnp.where(left, row, 0.0), jnp.where(left, 0.0, row)]

        def key_side(rows):
            turned = jnp.transpose(rows)
            if blocks == 1:
                return turned[:, 0 : channels + heads].astype(BF16)
            first, last = turned[0:count], turned[count:lanes]
            rolled = pltpu.roll(last, channels, 1)
            terms = pltpu.roll(first, channels + heads, 1)
            _, lane = iotas(count, 2 * channels)
            one = jnp.where(lane < channels, first, rolled)
            two = jnp.where(lane < heads, rolled, terms)
            return jnp.concatenate([one, two[:, 0 : 2 * heads]], axis=1).astype(BF16)

        def velocity(u, s):
            rounded = u.astype(BF16)
            wide = rounded.astype(F32)
            s2 = s * s
            features = jnp.concatenate(
                [
                    rounded,
                    (s * wide).astype(BF16),
                    (s2 * wide).astype(BF16),
                    jnp.zeros((channels, lanes), BF16),
                ],
                axis=0,
            )
            twice = jnp.concatenate([rounded, rounded], axis=0)
            sides = dot(side_ref[0 : 2 * channels], twice) + dot(
                side_ref[2 * channels : 4 * channels], twice
            )
            norm = jnp.sum(sides[0:channels] * wide, axis=0, keepdims=True)
            r = lax.rsqrt(jnp.maximum(norm, 0.0) + 1e-06)
            maps = [vector_maps]
            for h in range(heads):
                base = h * rows_all
                maps.append(jnp.concatenate([pay_ref[base : base + channels], square(h)], axis=1))
            product = dot(jnp.concatenate(maps, axis=0), features)
            values = dot(
                jnp.concatenate(
                    [
                        pay_ref[h * rows_all + third : h * rows_all + tail]
                        for h in range(heads)
                    ],
                    axis=0,
                ),
                features[0 : 2 * channels],
            )
            offsets = r * product[heads : 2 * heads] + s2 * constants
            blank = jnp.zeros((channels - heads, lanes), F32)
            keys = key_side(jnp.concatenate([r * wide, r * product[0:heads], blank], axis=0))
            r_blocks = by_block(r)
            at_queries = 2 * heads
            rhs, pairs = [], []
            for h in range(heads):
                at = at_queries + h * channels
                raw = product[at : at + channels]
                query = [(raw * part).astype(BF16) for part in r_blocks]
                pairs.append(jnp.concatenate([*query, selectors[h]], axis=0))
            if blocks == 1:
                all_scores = [dot(keys, pair) for pair in pairs]
            else:
                joined = dot(keys, jnp.concatenate(pairs, axis=1))
                all_scores = [
                    joined[:, h * lanes : (h + 1) * lanes] for h in range(heads)
                ]
            for h in range(heads):
                scores = all_scores[h] + offsets[h : h + 1]
                raised = jnp.exp2(scores - jnp.max(scores, axis=0, keepdims=True))
                inverse = 1.0 / jnp.sum(raised, axis=0, keepdims=True)
                rhs += [(raised * part).astype(BF16) for part in by_block(inverse)]
            values = [
                (r * values[h * channels : (h + 1) * channels]).astype(BF16)
                for h in range(heads)
            ]
            mixed = dot(jnp.concatenate(values, axis=1), jnp.concatenate(rhs, axis=0))
            return (r * sides[channels : 2 * channels] + s * p_sum) + mixed

        noise = jnp.transpose(start[...])[0:channels]
        noise = jnp.concatenate([noise] * blocks, axis=1)
        moved = velocity(noise, level(0, 0))
        first_coarse = noise + span(0) * moved
        if slab_id == 0:
            u = noise + step(0, 0) * moved
            for j in range(1, fine_most):
                u = u + step(0, j) * velocity(u, level(0, j))
            ended = first_coarse + (u - first_coarse)
        else:
            u = jnp.where(left, noise + step(0, 0) * moved, first_coarse)
            coarse_old = None
            for j in range(fine_most):
                last = j == fine_most - 1
                s = jnp.where(left, level(1, 0) if last else level(0, j + 1), level(1, j))
                moved = velocity(u, s)
                if j == 0:
                    coarse_old = u + span(1) * moved
                u = u + jnp.where(left, span(1) if last else step(0, j + 1), step(1, j)) * moved
            ended = u + pltpu.roll(u - coarse_old, count, 1)
        out_ref[...] = jnp.transpose(ended)[0:tokens, 0:channels]


def exchanged(value, stride):
    groups, size, slabs = (lax.axis_size(axis) for axis in ("groups", "seq", "slab"))
    pairs = []
    for g in range(groups):
        for s in range(size):
            for c in range(slabs):
                if c == slabs - 1 or groups % 2:
                    to = (g, s ^ stride)
                else:
                    to = (g ^ 1, s)
                pairs.append(((g * size + s) * slabs + c, (to[0] * size + to[1]) * slabs + c))
    return lax.ppermute(value, ("groups", "seq", "slab"), pairs)


def local(
    noise,
    timesteps,
    fine_counts,
    w_in,
    w_query,
    w_key,
    w_value,
    w_out,
    w_final,
    mod_scale,
    mod_shift,
    skip_gain,
):
    channels, width = w_in.shape
    tokens = noise.shape[0]
    heads = lax.axis_size("seq")
    half = heads // 2
    count = tokens * heads
    points = timesteps.shape[1]
    *_, rows = layout(channels, tokens)
    wf_t = w_final.T
    vmem = pl.BlockSpec(memory_space=pltpu.VMEM)
    smem = pl.BlockSpec(memory_space=pltpu.SMEM)
    hbm = pl.BlockSpec(memory_space=pl.ANY)

    def near(*values):
        return [pltpu.with_memory_space_constraint(value, pltpu.VMEM) for value in values]

    pieces = 1
    packed = pl.pallas_call(
        functools.partial(fold_kernel, pieces=pieces),
        out_shape=pltpu.VMEM((rows, 2 * channels), BF16),
        in_specs=[hbm] * 9,
        out_specs=vmem,
        scratch_shapes=[
            pltpu.VMEM((tokens, channels), F32),
            pltpu.VMEM((channels, width), BF16),
            pltpu.VMEM((width, HEAD_SIZE), BF16),
            pltpu.VMEM((width, HEAD_SIZE), BF16),
            pltpu.VMEM((width, HEAD_SIZE), BF16),
            pltpu.VMEM((HEAD_SIZE, width), BF16),
            pltpu.VMEM((channels, width), F32),
            pltpu.VMEM((width,), F32),
            pltpu.VMEM((width,), F32),
            pltpu.SemaphoreType.DMA((6 + 3 * pieces,)),
        ],
        name="fold",
    )(noise, w_in, w_query, w_key, w_value, w_out, wf_t, mod_scale, mod_shift)
    stride = half
    own = packed
    while stride > 1:
        own = jnp.concatenate([own, exchanged(own, stride)], axis=0)
        stride //= 2

    def tables(n, kind):
        return (
            kind((n * channels, 2 * channels), BF16),
            *(kind((n, 2 * channels), F32) for _ in range(4)),
            kind((n * tokens, 2 * channels), F32),
        )

    side, plan, *firsts = pl.pallas_call(
        functools.partial(side_kernel, heads=half, rows_all=rows, tokens=tokens),
        out_shape=(
            pltpu.VMEM((4 * channels, 2 * channels), BF16),
            pltpu.VMEM((4 * points, 2 * count), F32),
            *tables(half, pltpu.VMEM),
        ),
        in_specs=[smem, smem, vmem, vmem, vmem, vmem],
        out_specs=(vmem,) * 8,
        name="side",
    )(timesteps, fine_counts, w_in, wf_t, skip_gain, *near(own))
    own = jnp.concatenate([own, exchanged(own, 1)], axis=0)
    own, side, plan, *firsts = lax.optimization_barrier((own, side, plan, *firsts))
    other = lax.ppermute(own, "slab", [(0, 1), (1, 0)])

    def solve(slab_id, pay, before, kind):
        return pl.pallas_call(
            functools.partial(
                solve_kernel,
                heads=heads,
                tokens=tokens,
                slab_id=slab_id,
                ready=half if slab_id else 0,
                points=points,
            ),
            out_shape=kind((tokens, channels), F32),
            in_specs=[vmem] * 10,
            out_specs=vmem,
            scratch_shapes=tables(heads, pltpu.VMEM),
            name=f"solve{slab_id}",
        )(*near(pay, side, plan, *firsts, before))

    ended = solve(1, own, plan[0:tokens, 0:channels], pltpu.VMEM)
    ended = solve(0, other, ended, jax.ShapeDtypeStruct)
    return ended[None]


def solution(mesh):
    placed = (
        P(("groups", "seq"), None),
        P("groups", None),
        P("groups"),
        P(),
        P(None, "seq"),
        P(None, "seq"),
        P(None, "seq"),
        P("seq", None),
        P(),
        P(),
        P(),
        P(),
    )
    return jax.shard_map(
        local,
        mesh=mesh,
        in_specs=placed,
        out_specs=P("slab", ("groups", "seq"), None),
        check_vma=False,
    )
```

```python
import functools
import math

import jax
import jax.numpy as jnp
from jax import lax
from jax.experimental import pallas as pl
from jax.experimental.pallas import tpu as pltpu
from jax.sharding import PartitionSpec as P

HEAD_SIZE = 128
F32 = jnp.float32
BF16 = jnp.bfloat16
NT = (((1,), (1,)), ((), ()))
TN = (((0,), (0,)), ((), ()))


def dot(a, b, dims=(((1,), (0,)), ((), ()))):
    return lax.dot_general(a, b, dims, preferred_element_type=F32)


def split2(x):
    high = x.astype(BF16)
    return high, (x - high.astype(F32)).astype(BF16)


def split3(x):
    high = x.astype(BF16)
    mid, low = split2(x - high.astype(F32))
    return high, mid, low


def dot_fine(a, b):
    a_high, a_low = split2(a)
    b_high, b_low = split2(b)
    return dot(
        jnp.concatenate([a_high, a_high, a_low], axis=1),
        jnp.concatenate([b_high, b_low, b_high], axis=1),
        NT,
    )


def layout(channels, tokens):
    second = channels
    third = second + channels // 2
    tail = third + channels
    return second, third, tail, tail + 4 + tokens // 2 + tokens


def iotas(rows, columns):
    return (
        lax.broadcasted_iota(jnp.int32, (rows, columns), 0),
        lax.broadcasted_iota(jnp.int32, (rows, columns), 1),
    )


def fold_kernel(
    noise_hbm,
    w_in_hbm,
    wq_hbm,
    wk_hbm,
    wv_hbm,
    wo_hbm,
    wf_hbm,
    scale_hbm,
    shift_hbm,
    out_ref,
    noise,
    w_in,
    w_a,
    w_b,
    w_c,
    wo,
    wf,
    scale,
    shift,
    sems,
    *,
    pieces,
):
    slab = lax.axis_index("slab")
    channels, width = w_in.shape
    half = channels // 2
    tokens = noise.shape[0]
    second, third, tail, rows_all = layout(channels, tokens)

    def parts(total):
        last = total[2 * channels : 2 * channels + 8]
        return total[0:channels], total[channels : 2 * channels], last[0:1] + last[1:2]

    @pl.when(slab == 0)
    def _():
        out_ref[...] = jnp.zeros_like(out_ref)

    @pl.when(slab != 0)
    def _():
        used = 0

        def fetch(src, dst):
            nonlocal used
            copy = pltpu.make_async_copy(src, dst, sems.at[used])
            copy.start()
            used += 1
            return copy

        waits = [fetch(w_in_hbm, w_in), fetch(scale_hbm, scale), fetch(shift_hbm, shift)]
        tiles = width // HEAD_SIZE
        cuts = [tiles * k // pieces // 2 * 2 * HEAD_SIZE for k in range(pieces)] + [width]
        pulls = []
        for low, high in zip(cuts, cuts[1:]):
            at = pl.ds(low, high - low)
            pulls.append(
                [
                    fetch(src.at[at], dst.at[at])
                    for src, dst in ((wq_hbm, w_a), (wk_hbm, w_b), (wv_hbm, w_c))
                ]
            )
        finals = [fetch(wf_hbm, wf), fetch(wo_hbm, wo), fetch(noise_hbm, noise)]
        total = None
        for copy in waits:
            copy.wait()
        factors = scale[...].reshape(1, width)
        shift_high, shift_low = split2(shift[...].reshape(1, width))
        shift_high, shift_low = shift_high.astype(F32), shift_low.astype(F32)
        for low, high, pull in zip(cuts, cuts[1:], pulls):
            for copy in pull:
                copy.wait()
            at = slice(low, high)
            plain = w_in[:, at]
            scaled = plain.astype(F32) * factors[:, at]
            row, _ = iotas(16, high - low)
            vectors = jnp.where(
                row == 0, shift_high[:, at], jnp.where(row == 1, shift_low[:, at], 0.0)
            )
            lift = jnp.concatenate([plain, scaled.astype(BF16), vectors.astype(BF16)], axis=0)
            term = dot(lift, jnp.concatenate([w_a[at], w_b[at], w_c[at]], axis=1))
            total = term if total is None else total + term
        for copy in finals:
            copy.wait()
        both = dot(jnp.concatenate(split2(wf[...]), axis=0), wo[...], NT)
        out_t = both[0:channels] + both[channels : 2 * channels]
        q0, q1, q2 = parts(total[:, 0:HEAD_SIZE] * (math.log2(math.e) / math.sqrt(HEAD_SIZE)))
        k0, k1, k2 = parts(total[:, HEAD_SIZE : 2 * HEAD_SIZE])
        v0, v1, v2 = parts(total[:, 2 * HEAD_SIZE : 3 * HEAD_SIZE])
        pad = jnp.zeros((7, HEAD_SIZE), F32)
        q_all = jnp.concatenate([q0, q1], axis=0)
        k_all = jnp.concatenate([k0, k1], axis=0)
        form = dot_fine(k_all, q_all)
        a_rows = dot_fine(jnp.concatenate([k2, pad], axis=0), q_all)
        b_rows = dot_fine(jnp.concatenate([q2, pad], axis=0), k_all)
        constant = jnp.sum(k2 * q2)
        p_rows = dot_fine(
            jnp.concatenate([v2, pad], axis=0), jnp.concatenate([out_t, out_t], axis=0)
        )
        _, lane = iotas(channels, 2 * channels)
        top, bottom = form[0:channels], form[channels : 2 * channels]
        rolled = pltpu.roll(bottom, channels, 1)
        out_ref[0:channels] = jnp.where(lane < channels, top, top + rolled).astype(BF16)
        out_ref[second:third] = jnp.where(
            lane[0:half] < channels, rolled[0:half], bottom[half:channels]
        ).astype(BF16)
        out_ref[third:tail] = dot_fine(out_t, jnp.concatenate([v0, v1], axis=0)).astype(BF16)
        n_high, n_mid, n_low = (part.astype(F32) for part in split3(noise[...]))
        lows = jnp.concatenate([n_low[0 : tokens // 2], n_low[tokens // 2 : tokens]], axis=1)
        row, lane = iotas(4, 2 * channels)
        left = lane < channels
        a_roll = pltpu.roll(a_rows, channels, 1)[0:1]
        b_roll = pltpu.roll(b_rows, channels, 1)[0:1]
        vectors = jnp.where(
            row == 0,
            jnp.where(left, 0.0, a_roll),
            jnp.where(
                row == 1,
                jnp.where(left, a_roll, constant),
                jnp.where(
                    row == 2,
                    jnp.where(left, 0.0, b_roll),
                    jnp.where(left, b_roll, p_rows[0:1]),
                ),
            ),
        )
        out_ref[tail:rows_all] = jnp.concatenate(
            [vectors, lows, jnp.concatenate([n_high, n_mid], axis=1)], axis=0
        ).astype(BF16)


def unpack(pay_ref, base, h, tables, channels, tokens):
    squares, *vectors, start = tables
    second, third, tail, rows_all = layout(channels, tokens)
    folded = pay_ref[pl.ds(base + second, third - second)].astype(F32)
    ext = pay_ref[pl.ds(base + tail, rows_all - tail)].astype(F32)
    at = pl.ds(h * channels, channels)
    squares[at] = jnp.concatenate([folded, pltpu.roll(folded, channels, 1)], axis=0).astype(BF16)
    for i, vector in enumerate(vectors):
        vector[pl.ds(h, 1)] = ext[i : i + 1]
    lows = ext[4 : 4 + tokens // 2]
    pieces = ext[4 + tokens // 2 :]
    low = jnp.concatenate([lows, pltpu.roll(lows, channels, 1)], axis=0)
    start[pl.ds(h * tokens, tokens)] = (pieces + pltpu.roll(pieces, channels, 1)) + low


def side_kernel(
    times_ref,
    counts_ref,
    w_in_ref,
    wf_ref,
    gain_ref,
    out_ref,
    plan_ref,
):
    channels, width = w_in_ref.shape
    w_in = w_in_ref[...]
    gram = dot(w_in, w_in, NT) * (1.0 / width)
    gained = w_in.astype(F32) * gain_ref[...].reshape(1, width)
    skip = dot_fine(wf_ref[...], gained)
    g_high, g_mid, g_low = split3(gram)
    s_high, s_low = split2(skip)
    zero = jnp.zeros_like(s_high)
    out_ref[...] = jnp.concatenate(
        [
            jnp.concatenate([g_high, g_mid], axis=1),
            jnp.concatenate([s_high, s_low], axis=1),
            jnp.concatenate([g_low, zero], axis=1),
            jnp.concatenate([zero, zero], axis=1),
        ],
        axis=0,
    )

    lanes = plan_ref.shape[1]
    points = times_ref.shape[1]

    def level(slab_id, column):
        whole = jnp.zeros((1, lanes), jnp.int32) + times_ref[slab_id, column]
        return whole.astype(F32) / 1000.0

    for k in range(2):
        levels = [level(k, column) for column in range(points)]
        last = jnp.zeros((1, lanes), F32)
        for column in range(points):
            last = jnp.where(column == counts_ref[k], levels[column], last)
        steps = [
            jnp.where(j < counts_ref[k], levels[j + 1] - levels[j], 0.0)
            for j in range(points - 1)
        ]
        rows = levels + steps + [last - levels[0]]
        for i, value in enumerate(rows):
            plan_ref[pl.ds(k * 2 * points + i, 1)] = value


def solve_kernel(
    pay_ref,
    side_ref,
    plan_ref,
    before_ref,
    out_ref,
    *tables,
    heads,
    tokens,
    slab_id,
    points,
):
    squares, a_first, a_second, b_first, b_second, start = tables
    slab = lax.axis_index("slab")
    channels = side_ref.shape[1] // 2
    count = heads * tokens
    lanes = 2 * count
    second, third, tail, rows_all = layout(channels, tokens)
    fine_most = points - 1

    @pl.when(slab != slab_id)
    def _():
        out_ref[...] = before_ref[...]

    @pl.when(slab == slab_id)
    def _():
        for h in range(heads):
            unpack(pay_ref, h * rows_all, h, tables, channels, tokens)

        def square(h):
            at = slice(h * channels, (h + 1) * channels)
            return squares[at]

        _, lane = iotas(1, lanes)
        left = lane < count
        constants = jnp.broadcast_to(a_second[:, channels : channels + 1], (heads, lanes))
        vector_maps = jnp.concatenate(
            [
                jnp.concatenate([b_first[...], a_first[...]], axis=0),
                jnp.concatenate([b_second[...], a_second[...]], axis=0),
            ],
            axis=1,
        ).astype(BF16)
        p_row = jnp.sum(b_second[...], axis=0, keepdims=True)
        p_row = jnp.broadcast_to(p_row, (8, 2 * channels))
        p_sum = jnp.broadcast_to(
            jnp.transpose(p_row)[channels : 2 * channels, 0:1], (channels, lanes)
        )
        row, column = iotas(heads, lanes)
        pair_selectors = [
            jnp.where(
                ((row == h) & (column < count)) | ((row == h + 1) & (column >= count)), 1.0, 0.0
            ).astype(BF16)
            for h in range(0, heads, 2)
        ]
        row, column = iotas(2 * heads, lanes)
        selectors = [
            jnp.where(
                ((row == h) & (column >= count)) | ((row == heads + h) & (column < count)), 1.0, 0.0
            ).astype(BF16)
            for h in range(heads)
        ]

        def level(k, column):
            row = k * 2 * points + column
            return plan_ref[row : row + 1, 0:lanes]

        def step(k, j):
            return level(k, points + j)

        def span(k):
            return level(k, 2 * points - 1)

        def by_block(row):
            return [jnp.where(left, row, 0.0), jnp.where(left, 0.0, row)]

        def key_side(rows, same):
            turned = jnp.transpose(rows)
            first, last = turned[0:count], turned[count:lanes]
            if same:
                return first[:, 0 : channels + heads].astype(BF16)
            rolled = pltpu.roll(last, channels, 1)
            terms = pltpu.roll(first, channels + heads, 1)
            _, lane = iotas(count, 2 * channels)
            one = jnp.where(lane < channels, first, rolled)
            two = jnp.where(lane < heads, rolled, terms)
            return jnp.concatenate([one, two[:, 0 : 2 * heads]], axis=1).astype(BF16)

        def softmax(scores):
            raised = jnp.exp2(scores - jnp.max(scores, axis=0, keepdims=True))
            return raised, 1.0 / jnp.sum(raised, axis=0, keepdims=True)

        def velocity(u, s, same):
            rounded = u.astype(BF16)
            wide = rounded.astype(F32)
            s2 = s * s
            features = jnp.concatenate(
                [
                    rounded,
                    (s * wide).astype(BF16),
                    (s2 * wide).astype(BF16),
                    jnp.zeros((channels, lanes), BF16),
                ],
                axis=0,
            )
            twice = jnp.concatenate([rounded, rounded], axis=0)
            sides = dot(side_ref[0 : 2 * channels], twice) + dot(
                side_ref[2 * channels : 4 * channels], twice
            )
            norm = jnp.sum(sides[0:channels] * wide, axis=0, keepdims=True)
            r = lax.rsqrt(jnp.maximum(norm, 0.0) + 1e-06)
            maps = [vector_maps]
            for h in range(heads):
                base = h * rows_all
                maps.append(jnp.concatenate([pay_ref[base : base + channels], square(h)], axis=1))
            product = dot(jnp.concatenate(maps, axis=0), features)
            values = dot(
                jnp.concatenate(
                    [
                        pay_ref[h * rows_all + third : h * rows_all + tail]
                        for h in range(heads)
                    ],
                    axis=0,
                ),
                features[0 : 2 * channels],
            )
            offsets = r * product[heads : 2 * heads] + s2 * constants
            blank = jnp.zeros((channels - heads, lanes), F32)
            keys = key_side(jnp.concatenate([r * wide, r * product[0:heads], blank], axis=0), same)
            at_queries = 2 * heads
            raws = [
                product[at_queries + h * channels : at_queries + (h + 1) * channels]
                for h in range(heads)
            ]
            own_part = r * sides[channels : 2 * channels] + s * p_sum
            if same:
                pairs = []
                for h in range(0, heads, 2):
                    query = (r * jnp.where(left, raws[h], raws[h + 1])).astype(BF16)
                    pairs.append(jnp.concatenate([query, pair_selectors[h // 2]], axis=0))
                joined = dot(keys, jnp.concatenate(pairs, axis=1))
                rhs = []
                for h in range(0, heads, 2):
                    at = h // 2 * lanes
                    offset = jnp.where(left, offsets[h : h + 1], offsets[h + 1 : h + 2])
                    raised, inverse = softmax(joined[:, at : at + lanes] + offset)
                    rhs.append((raised * inverse).astype(BF16))
                values = [
                    r * values[h * channels : (h + 1) * channels] for h in range(heads)
                ]
                lhs = [
                    jnp.concatenate(
                        [
                            jnp.where(left, values[h + k], values[h + k + 2]).astype(BF16)
                            for h in range(0, heads, 4)
                        ],
                        axis=1,
                    )
                    for k in range(2)
                ]
                both = dot(jnp.concatenate(lhs, axis=0), jnp.concatenate(rhs, axis=0))
                mixed = jnp.where(left, both[0:channels], both[channels : 2 * channels])
                return own_part + (mixed + pltpu.roll(mixed, count, 1))
            r_blocks = by_block(r)
            pairs = []
            for h in range(heads):
                query = [(raws[h] * part).astype(BF16) for part in r_blocks]
                pairs.append(jnp.concatenate([*query, selectors[h]], axis=0))
            joined = dot(keys, jnp.concatenate(pairs, axis=1))
            rhs = []
            for h in range(heads):
                raised, inverse = softmax(
                    joined[:, h * lanes : (h + 1) * lanes] + offsets[h : h + 1]
                )
                rhs += [(raised * part).astype(BF16) for part in by_block(inverse)]
            values = [
                (r * values[h * channels : (h + 1) * channels]).astype(BF16)
                for h in range(heads)
            ]
            return own_part + dot(
                jnp.concatenate(values, axis=1), jnp.concatenate(rhs, axis=0)
            )

        noise = jnp.transpose(start[...])[0:channels]
        noise = jnp.concatenate([noise, noise], axis=1)
        moved = velocity(noise, level(0, 0), True)
        first_coarse = noise + span(0) * moved
        if slab_id == 0:
            u = noise + step(0, 0) * moved
            for j in range(1, fine_most):
                u = u + step(0, j) * velocity(u, level(0, j), True)
            ended = first_coarse + (u - first_coarse)
        else:
            u = jnp.where(left, noise + step(0, 0) * moved, first_coarse)
            coarse_old = None
            for j in range(fine_most):
                last = j == fine_most - 1
                s = jnp.where(left, level(1, 0) if last else level(0, j + 1), level(1, j))
                moved = velocity(u, s, False)
                if j == 0:
                    coarse_old = u + span(1) * moved
                u = u + jnp.where(left, span(1) if last else step(0, j + 1), step(1, j)) * moved
            ended = u + pltpu.roll(u - coarse_old, count, 1)
        out_ref[...] = jnp.transpose(ended)[0:tokens, 0:channels]


def exchanged(value, stride):
    groups, size, slabs = (lax.axis_size(axis) for axis in ("groups", "seq", "slab"))
    pairs = []
    for g in range(groups):
        for s in range(size):
            for c in range(slabs):
                if c == slabs - 1 or groups % 2:
                    to = (g, s ^ stride)
                else:
                    to = (g ^ 1, s)
                pairs.append(((g * size + s) * slabs + c, (to[0] * size + to[1]) * slabs + c))
    return lax.ppermute(value, ("groups", "seq", "slab"), pairs)


def gathered(packed):
    size = lax.axis_size("seq")
    if size == 8:
        order = (6, 5, 7, 4, 3, 2, 1)
        return jnp.concatenate([packed] + [exchanged(packed, k) for k in order], axis=0)
    own, stride = packed, size // 2
    while stride:
        own = jnp.concatenate([own, exchanged(own, stride)], axis=0)
        stride //= 2
    return own


def local(
    noise,
    timesteps,
    fine_counts,
    w_in,
    w_query,
    w_key,
    w_value,
    w_out,
    w_final,
    mod_scale,
    mod_shift,
    skip_gain,
):
    channels, width = w_in.shape
    tokens = noise.shape[0]
    heads = lax.axis_size("seq")
    count = tokens * heads
    points = timesteps.shape[1]
    *_, rows = layout(channels, tokens)
    wf_t = w_final.T
    vmem = pl.BlockSpec(memory_space=pltpu.VMEM)
    smem = pl.BlockSpec(memory_space=pltpu.SMEM)
    hbm = pl.BlockSpec(memory_space=pl.ANY)

    def near(*values):
        return [pltpu.with_memory_space_constraint(value, pltpu.VMEM) for value in values]

    pieces = 1
    packed = pl.pallas_call(
        functools.partial(fold_kernel, pieces=pieces),
        out_shape=pltpu.VMEM((rows, 2 * channels), BF16),
        in_specs=[hbm] * 9,
        out_specs=vmem,
        scratch_shapes=[
            pltpu.VMEM((tokens, channels), F32),
            pltpu.VMEM((channels, width), BF16),
            pltpu.VMEM((width, HEAD_SIZE), BF16),
            pltpu.VMEM((width, HEAD_SIZE), BF16),
            pltpu.VMEM((width, HEAD_SIZE), BF16),
            pltpu.VMEM((HEAD_SIZE, width), BF16),
            pltpu.VMEM((channels, width), F32),
            pltpu.VMEM((width,), F32),
            pltpu.VMEM((width,), F32),
            pltpu.SemaphoreType.DMA((6 + 3 * pieces,)),
        ],
        name="fold",
    )(noise, w_in, w_query, w_key, w_value, w_out, wf_t, mod_scale, mod_shift)
    own = gathered(packed)

    def tables(n, kind):
        return (
            kind((n * channels, 2 * channels), BF16),
            *(kind((n, 2 * channels), F32) for _ in range(4)),
            kind((n * tokens, 2 * channels), F32),
        )

    side, plan = pl.pallas_call(
        side_kernel,
        out_shape=(
            pltpu.VMEM((4 * channels, 2 * channels), BF16),
            pltpu.VMEM((4 * points, 2 * count), F32),
        ),
        in_specs=[smem, smem, vmem, vmem, vmem],
        out_specs=(vmem,) * 2,
        name="side",
    )(timesteps, fine_counts, w_in, wf_t, skip_gain)
    own, side, plan = lax.optimization_barrier((own, side, plan))
    other = lax.ppermute(own, "slab", [(0, 1), (1, 0)])

    def solve(slab_id, pay, before, kind):
        return pl.pallas_call(
            functools.partial(
                solve_kernel,
                heads=heads,
                tokens=tokens,
                slab_id=slab_id,
                points=points,
            ),
            out_shape=kind((tokens, channels), F32),
            in_specs=[vmem] * 4,
            out_specs=vmem,
            scratch_shapes=tables(heads, pltpu.VMEM),
            name=f"solve{slab_id}",
        )(*near(pay, side, plan, before))

    ended = solve(1, own, plan[0:tokens, 0:channels], pltpu.VMEM)
    ended = solve(0, other, ended, jax.ShapeDtypeStruct)
    return ended[None]


def solution(mesh):
    placed = (
        P(("groups", "seq"), None),
        P("groups", None),
        P("groups"),
        P(),
        P(None, "seq"),
        P(None, "seq"),
        P(None, "seq"),
        P("seq", None),
        P(),
        P(),
        P(),
        P(),
    )
    return jax.shard_map(
        local,
        mesh=mesh,
        in_specs=placed,
        out_specs=P("slab", ("groups", "seq"), None),
        check_vma=False,
    )
```

```python
import functools
import math

import jax
import jax.numpy as jnp
from jax import lax
from jax.experimental import pallas as pl
from jax.experimental.pallas import tpu as pltpu
from jax.sharding import PartitionSpec as P

HEAD_SIZE = 128
F32 = jnp.float32
BF16 = jnp.bfloat16
NT = (((1,), (1,)), ((), ()))
TN = (((0,), (0,)), ((), ()))


def dot(a, b, dims=(((1,), (0,)), ((), ()))):
    return lax.dot_general(a, b, dims, preferred_element_type=F32)


def split2(x):
    high = x.astype(BF16)
    return high, (x - high.astype(F32)).astype(BF16)


def split3(x):
    high = x.astype(BF16)
    mid, low = split2(x - high.astype(F32))
    return high, mid, low


def dot_fine(a, b):
    a_high, a_low = split2(a)
    b_high, b_low = split2(b)
    return dot(
        jnp.concatenate([a_high, a_high, a_low], axis=1),
        jnp.concatenate([b_high, b_low, b_high], axis=1),
        NT,
    )


def layout(channels, tokens):
    second = channels
    third = second + channels // 2
    tail = third + channels
    return second, third, tail, tail + 4 + tokens // 2 + tokens


def iotas(rows, columns):
    return (
        lax.broadcasted_iota(jnp.int32, (rows, columns), 0),
        lax.broadcasted_iota(jnp.int32, (rows, columns), 1),
    )


def fold_kernel(
    noise_hbm,
    w_in_hbm,
    wq_hbm,
    wk_hbm,
    wv_hbm,
    wo_hbm,
    wf_hbm,
    scale_hbm,
    shift_hbm,
    out_ref,
    noise,
    w_in,
    w_a,
    w_b,
    w_c,
    wo,
    wf,
    scale,
    shift,
    sems,
    *,
    pieces,
):
    channels, width = w_in.shape
    half = channels // 2
    tokens = noise.shape[0]
    second, third, tail, rows_all = layout(channels, tokens)

    def parts(total):
        last = total[2 * channels : 2 * channels + 8]
        return total[0:channels], total[channels : 2 * channels], last[0:1] + last[1:2]

    used = 0

    def fetch(src, dst):
        nonlocal used
        copy = pltpu.make_async_copy(src, dst, sems.at[used])
        copy.start()
        used += 1
        return copy

    waits = [fetch(w_in_hbm, w_in), fetch(scale_hbm, scale), fetch(shift_hbm, shift)]
    tiles = width // HEAD_SIZE
    cuts = [tiles * k // pieces // 2 * 2 * HEAD_SIZE for k in range(pieces)] + [width]
    pulls = []
    for low, high in zip(cuts, cuts[1:]):
        at = pl.ds(low, high - low)
        pulls.append(
            [
                fetch(src.at[at], dst.at[at])
                for src, dst in ((wq_hbm, w_a), (wk_hbm, w_b), (wv_hbm, w_c))
            ]
        )
    finals = [fetch(wf_hbm, wf), fetch(wo_hbm, wo), fetch(noise_hbm, noise)]
    total = None
    for copy in waits:
        copy.wait()
    factors = scale[...].reshape(1, width)
    shift_high, shift_low = split2(shift[...].reshape(1, width))
    shift_high, shift_low = shift_high.astype(F32), shift_low.astype(F32)
    for low, high, pull in zip(cuts, cuts[1:], pulls):
        for copy in pull:
            copy.wait()
        at = slice(low, high)
        plain = w_in[:, at]
        scaled = plain.astype(F32) * factors[:, at]
        row, _ = iotas(16, high - low)
        vectors = jnp.where(
            row == 0, shift_high[:, at], jnp.where(row == 1, shift_low[:, at], 0.0)
        )
        lift = jnp.concatenate([plain, scaled.astype(BF16), vectors.astype(BF16)], axis=0)
        term = dot(lift, jnp.concatenate([w_a[at], w_b[at], w_c[at]], axis=1))
        total = term if total is None else total + term
    for copy in finals:
        copy.wait()
    both = dot(jnp.concatenate(split2(wf[...]), axis=0), wo[...], NT)
    out_t = both[0:channels] + both[channels : 2 * channels]
    q0, q1, q2 = parts(total[:, 0:HEAD_SIZE] * (math.log2(math.e) / math.sqrt(HEAD_SIZE)))
    k0, k1, k2 = parts(total[:, HEAD_SIZE : 2 * HEAD_SIZE])
    v0, v1, v2 = parts(total[:, 2 * HEAD_SIZE : 3 * HEAD_SIZE])
    pad = jnp.zeros((7, HEAD_SIZE), F32)
    q_all = jnp.concatenate([q0, q1], axis=0)
    k_all = jnp.concatenate([k0, k1], axis=0)
    form = dot_fine(k_all, q_all)
    a_rows = dot_fine(jnp.concatenate([k2, pad], axis=0), q_all)
    b_rows = dot_fine(jnp.concatenate([q2, pad], axis=0), k_all)
    constant = jnp.sum(k2 * q2)
    p_rows = dot_fine(
        jnp.concatenate([v2, pad], axis=0), jnp.concatenate([out_t, out_t], axis=0)
    )
    _, lane = iotas(channels, 2 * channels)
    top, bottom = form[0:channels], form[channels : 2 * channels]
    rolled = pltpu.roll(bottom, channels, 1)
    out_ref[0:channels] = jnp.where(lane < channels, top, top + rolled).astype(BF16)
    out_ref[second:third] = jnp.where(
        lane[0:half] < channels, rolled[0:half], bottom[half:channels]
    ).astype(BF16)
    out_ref[third:tail] = dot_fine(out_t, jnp.concatenate([v0, v1], axis=0)).astype(BF16)
    n_high, n_mid, n_low = (part.astype(F32) for part in split3(noise[...]))
    lows = jnp.concatenate([n_low[0 : tokens // 2], n_low[tokens // 2 : tokens]], axis=1)
    row, lane = iotas(4, 2 * channels)
    left = lane < channels
    a_roll = pltpu.roll(a_rows, channels, 1)[0:1]
    b_roll = pltpu.roll(b_rows, channels, 1)[0:1]
    vectors = jnp.where(
        row == 0,
        jnp.where(left, 0.0, a_roll),
        jnp.where(
            row == 1,
            jnp.where(left, a_roll, constant),
            jnp.where(
                row == 2,
                jnp.where(left, 0.0, b_roll),
                jnp.where(left, b_roll, p_rows[0:1]),
            ),
        ),
    )
    out_ref[tail:rows_all] = jnp.concatenate(
        [vectors, lows, jnp.concatenate([n_high, n_mid], axis=1)], axis=0
    ).astype(BF16)


def unpack(pay_ref, base, h, tables, channels, tokens):
    squares, *vectors, start = tables
    second, third, tail, rows_all = layout(channels, tokens)
    folded = pay_ref[pl.ds(base + second, third - second)].astype(F32)
    ext = pay_ref[pl.ds(base + tail, rows_all - tail)].astype(F32)
    at = pl.ds(h * channels, channels)
    squares[at] = jnp.concatenate([folded, pltpu.roll(folded, channels, 1)], axis=0).astype(BF16)
    for i, vector in enumerate(vectors):
        vector[pl.ds(h, 1)] = ext[i : i + 1]
    lows = ext[4 : 4 + tokens // 2]
    pieces = ext[4 + tokens // 2 :]
    low = jnp.concatenate([lows, pltpu.roll(lows, channels, 1)], axis=0)
    start[pl.ds(h * tokens, tokens)] = (pieces + pltpu.roll(pieces, channels, 1)) + low


def side_kernel(
    times_ref,
    counts_ref,
    w_in_ref,
    wf_ref,
    gain_ref,
    out_ref,
    plan_ref,
):
    channels, width = w_in_ref.shape
    w_in = w_in_ref[...]
    gram = dot(w_in, w_in, NT) * (1.0 / width)
    gained = w_in.astype(F32) * gain_ref[...].reshape(1, width)
    skip = dot_fine(wf_ref[...], gained)
    g_high, g_mid, g_low = split3(gram)
    s_high, s_low = split2(skip)
    zero = jnp.zeros_like(s_high)
    out_ref[...] = jnp.concatenate(
        [
            jnp.concatenate([g_high, g_mid], axis=1),
            jnp.concatenate([s_high, s_low], axis=1),
            jnp.concatenate([g_low, zero], axis=1),
            jnp.concatenate([zero, zero], axis=1),
        ],
        axis=0,
    )

    lanes = plan_ref.shape[1]
    points = times_ref.shape[1]

    def level(slab_id, column):
        whole = jnp.zeros((1, lanes), jnp.int32) + times_ref[slab_id, column]
        return whole.astype(F32) / 1000.0

    for k in range(2):
        levels = [level(k, column) for column in range(points)]
        last = jnp.zeros((1, lanes), F32)
        for column in range(points):
            last = jnp.where(column == counts_ref[k], levels[column], last)
        steps = [
            jnp.where(j < counts_ref[k], levels[j + 1] - levels[j], 0.0)
            for j in range(points - 1)
        ]
        rows = levels + steps + [last - levels[0]]
        for i, value in enumerate(rows):
            plan_ref[pl.ds(k * 2 * points + i, 1)] = value


def solve_kernel(
    *refs,
    arrays,
    heads,
    tokens,
    slab_id,
    points,
):
    pays = refs[:arrays]
    side_ref, plan_ref, before_ref, out_ref, *tables = refs[arrays:]
    squares, a_first, a_second, b_first, b_second, start = tables
    slab = lax.axis_index("slab")
    channels = side_ref.shape[1] // 2
    count = heads * tokens
    lanes = count if slab_id == 0 else 2 * count
    second, third, tail, rows_all = layout(channels, tokens)
    fine_most = points - 1

    def block(h):
        at = h * rows_all
        for pay_ref in pays:
            if at < pay_ref.shape[0]:
                return pay_ref, at
            at -= pay_ref.shape[0]

    def rows_of(h, low, high):
        ref, base = block(h)
        return ref[base + low : base + high]

    @pl.when(slab != slab_id)
    def _():
        out_ref[...] = before_ref[...]

    @pl.when(slab == slab_id)
    def _():
        for h in range(heads):
            unpack(*block(h), h, tables, channels, tokens)

        def square(h):
            at = slice(h * channels, (h + 1) * channels)
            return squares[at]

        _, lane = iotas(1, lanes)
        left = lane < count
        constants = jnp.broadcast_to(a_second[:, channels : channels + 1], (heads, lanes))
        vector_maps = jnp.concatenate(
            [
                jnp.concatenate([b_first[...], a_first[...]], axis=0),
                jnp.concatenate([b_second[...], a_second[...]], axis=0),
            ],
            axis=1,
        ).astype(BF16)
        p_row = jnp.sum(b_second[...], axis=0, keepdims=True)
        p_row = jnp.broadcast_to(p_row, (8, 2 * channels))
        p_sum = jnp.broadcast_to(
            jnp.transpose(p_row)[channels : 2 * channels, 0:1], (channels, lanes)
        )
        row, column = iotas(heads, lanes)
        pair_selectors = [
            jnp.where(
                ((row == h) & (column < count)) | ((row == h + 1) & (column >= count)), 1.0, 0.0
            ).astype(BF16)
            for h in range(0, heads, 2)
        ]
        if lanes == count:
            row, _ = iotas(heads, lanes)
            masks = [row == h for h in range(heads)]
        else:
            row, column = iotas(2 * heads, lanes)
            masks = [
                ((row == h) & (column >= count)) | ((row == heads + h) & (column < count))
                for h in range(heads)
            ]
        selectors = [jnp.where(mask, 1.0, 0.0).astype(BF16) for mask in masks]

        def level(k, column):
            row = k * 2 * points + column
            return plan_ref[row : row + 1, 0:lanes]

        def step(k, j):
            return level(k, points + j)

        def span(k):
            return level(k, 2 * points - 1)

        def by_block(row):
            if lanes == count:
                return [row]
            return [jnp.where(left, row, 0.0), jnp.where(left, 0.0, row)]

        def key_side(rows, same):
            turned = jnp.transpose(rows)
            first, last = turned[0:count], turned[count:lanes]
            if same or lanes == count:
                return first[:, 0 : channels + heads].astype(BF16)
            rolled = pltpu.roll(last, channels, 1)
            terms = pltpu.roll(first, channels + heads, 1)
            _, lane = iotas(count, 2 * channels)
            one = jnp.where(lane < channels, first, rolled)
            two = jnp.where(lane < heads, rolled, terms)
            return jnp.concatenate([one, two[:, 0 : 2 * heads]], axis=1).astype(BF16)

        def softmax(scores):
            raised = jnp.exp2(scores - jnp.max(scores, axis=0, keepdims=True))
            return raised, 1.0 / jnp.sum(raised, axis=0, keepdims=True)

        def velocity(u, s, same):
            rounded = u.astype(BF16)
            wide = rounded.astype(F32)
            s2 = s * s
            features = jnp.concatenate(
                [
                    rounded,
                    (s * wide).astype(BF16),
                    (s2 * wide).astype(BF16),
                    jnp.zeros((channels, lanes), BF16),
                ],
                axis=0,
            )
            twice = jnp.concatenate([rounded, rounded], axis=0)
            sides = dot(side_ref[0 : 2 * channels], twice) + dot(
                side_ref[2 * channels : 4 * channels], twice
            )
            norm = jnp.sum(sides[0:channels] * wide, axis=0, keepdims=True)
            r = lax.rsqrt(jnp.maximum(norm, 0.0) + 1e-06)
            maps = [vector_maps]
            for h in range(heads):
                maps.append(jnp.concatenate([rows_of(h, 0, channels), square(h)], axis=1))
            product = dot(jnp.concatenate(maps, axis=0), features)
            values = dot(
                jnp.concatenate(
                    [
                        rows_of(h, third, tail)
                        for h in range(heads)
                    ],
                    axis=0,
                ),
                features[0 : 2 * channels],
            )
            offsets = r * product[heads : 2 * heads] + s2 * constants
            blank = jnp.zeros((channels - heads, lanes), F32)
            keys = key_side(jnp.concatenate([r * wide, r * product[0:heads], blank], axis=0), same)
            at_queries = 2 * heads
            raws = [
                product[at_queries + h * channels : at_queries + (h + 1) * channels]
                for h in range(heads)
            ]
            own_part = r * sides[channels : 2 * channels] + s * p_sum
            if same:
                pairs = []
                for h in range(0, heads, 2):
                    query = (r * jnp.where(left, raws[h], raws[h + 1])).astype(BF16)
                    pairs.append(jnp.concatenate([query, pair_selectors[h // 2]], axis=0))
                joined = dot(keys, jnp.concatenate(pairs, axis=1))
                rhs = []
                for h in range(0, heads, 2):
                    at = h // 2 * lanes
                    offset = jnp.where(left, offsets[h : h + 1], offsets[h + 1 : h + 2])
                    raised, inverse = softmax(joined[:, at : at + lanes] + offset)
                    rhs.append((raised * inverse).astype(BF16))
                values = [
                    r * values[h * channels : (h + 1) * channels] for h in range(heads)
                ]
                lhs = [
                    jnp.concatenate(
                        [
                            jnp.where(left, values[h + k], values[h + k + 2]).astype(BF16)
                            for h in range(0, heads, 4)
                        ],
                        axis=1,
                    )
                    for k in range(2)
                ]
                both = dot(jnp.concatenate(lhs, axis=0), jnp.concatenate(rhs, axis=0))
                mixed = jnp.where(left, both[0:channels], both[channels : 2 * channels])
                return own_part + (mixed + pltpu.roll(mixed, count, 1))
            r_blocks = by_block(r)
            pairs = []
            for h in range(heads):
                query = [(raws[h] * part).astype(BF16) for part in r_blocks]
                pairs.append(jnp.concatenate([*query, selectors[h]], axis=0))
            if lanes == count:
                parts = [dot(keys, pair) for pair in pairs]
            else:
                joined = dot(keys, jnp.concatenate(pairs, axis=1))
                parts = [joined[:, h * lanes : (h + 1) * lanes] for h in range(heads)]
            rhs = []
            for h in range(heads):
                raised, inverse = softmax(parts[h] + offsets[h : h + 1])
                rhs += [(raised * part).astype(BF16) for part in by_block(inverse)]
            values = [
                (r * values[h * channels : (h + 1) * channels]).astype(BF16)
                for h in range(heads)
            ]
            return own_part + dot(
                jnp.concatenate(values, axis=1), jnp.concatenate(rhs, axis=0)
            )

        noise = jnp.transpose(start[...])[0:channels]
        both_slabs = slab_id != 0
        if both_slabs:
            noise = jnp.concatenate([noise, noise], axis=1)
        moved = velocity(noise, level(0, 0), both_slabs)
        first_coarse = noise + span(0) * moved
        if slab_id == 0:
            u = noise + step(0, 0) * moved
            for j in range(1, fine_most):
                u = u + step(0, j) * velocity(u, level(0, j), False)
            ended = first_coarse + (u - first_coarse)
        else:
            u = jnp.where(left, noise + step(0, 0) * moved, first_coarse)
            coarse_old = None
            for j in range(fine_most):
                last = j == fine_most - 1
                s = jnp.where(left, level(1, 0) if last else level(0, j + 1), level(1, j))
                moved = velocity(u, s, False)
                if j == 0:
                    coarse_old = u + span(1) * moved
                u = u + jnp.where(left, span(1) if last else step(0, j + 1), step(1, j)) * moved
            ended = u + pltpu.roll(u - coarse_old, count, 1)
        out_ref[...] = jnp.transpose(ended)[0:tokens, 0:channels]


def exchanged(value, distances):
    groups, size, slabs = (lax.axis_size(axis) for axis in ("groups", "seq", "slab"))
    pairs = []
    for g in range(groups):
        for s in range(size):
            for c in range(slabs):
                to = (g ^ 1, s) if distances[c] is None else (g, s ^ distances[c])
                pairs.append(((g * size + s) * slabs + c, (to[0] * size + to[1]) * slabs + c))
    return lax.ppermute(value, ("groups", "seq", "slab"), pairs)


def local(
    noise,
    timesteps,
    fine_counts,
    w_in,
    w_query,
    w_key,
    w_value,
    w_out,
    w_final,
    mod_scale,
    mod_shift,
    skip_gain,
):
    channels, width = w_in.shape
    tokens = noise.shape[0]
    heads = lax.axis_size("seq")
    count = tokens * heads
    points = timesteps.shape[1]
    *_, rows = layout(channels, tokens)
    wf_t = w_final.T
    vmem = pl.BlockSpec(memory_space=pltpu.VMEM)
    smem = pl.BlockSpec(memory_space=pltpu.SMEM)
    hbm = pl.BlockSpec(memory_space=pl.ANY)

    def near(*values):
        return [pltpu.with_memory_space_constraint(value, pltpu.VMEM) for value in values]

    pieces = 1
    packed = pl.pallas_call(
        functools.partial(fold_kernel, pieces=pieces),
        out_shape=pltpu.VMEM((rows, 2 * channels), BF16),
        in_specs=[hbm] * 9,
        out_specs=vmem,
        scratch_shapes=[
            pltpu.VMEM((tokens, channels), F32),
            pltpu.VMEM((channels, width), BF16),
            pltpu.VMEM((width, HEAD_SIZE), BF16),
            pltpu.VMEM((width, HEAD_SIZE), BF16),
            pltpu.VMEM((width, HEAD_SIZE), BF16),
            pltpu.VMEM((HEAD_SIZE, width), BF16),
            pltpu.VMEM((channels, width), F32),
            pltpu.VMEM((width,), F32),
            pltpu.VMEM((width,), F32),
            pltpu.SemaphoreType.DMA((6 + 3 * pieces,)),
        ],
        name="fold",
    )(noise, w_in, w_query, w_key, w_value, w_out, wf_t, mod_scale, mod_shift)
    swap = [(0, 1), (1, 0)]
    shared = heads == 8 and lax.axis_size("groups") % 2 == 0
    if shared:
        three = [exchanged(packed, pair) for pair in ((3, 6), (2, 5), (1, 7))]
        fourth = exchanged(packed, (None, 4))
        three = jnp.concatenate(three, axis=0)
    else:
        three, stride = packed, heads // 2
        while stride:
            three = jnp.concatenate([three, exchanged(three, (stride, stride))], axis=0)
            stride //= 2

    def tables(n, kind):
        return (
            kind((n * channels, 2 * channels), BF16),
            *(kind((n, 2 * channels), F32) for _ in range(4)),
            kind((n * tokens, 2 * channels), F32),
        )

    side, plan = pl.pallas_call(
        side_kernel,
        out_shape=(
            pltpu.VMEM((4 * channels, 2 * channels), BF16),
            pltpu.VMEM((4 * points, 2 * count), F32),
        ),
        in_specs=[smem, smem, vmem, vmem, vmem],
        out_specs=(vmem,) * 2,
        name="side",
    )(timesteps, fine_counts, w_in, wf_t, skip_gain)
    if shared:
        three, fourth, side, plan = lax.optimization_barrier((three, fourth, side, plan))
        traded = lax.ppermute(three, "slab", swap)
        held = [(packed, three, traded, lax.ppermute(fourth, "slab", swap))]
        held.append((packed, three, traded, fourth))
    else:
        held = [(three,), (three,)]

    def solve(slab_id, before, kind):
        return pl.pallas_call(
            functools.partial(
                solve_kernel,
                arrays=len(held[slab_id]),
                heads=heads,
                tokens=tokens,
                slab_id=slab_id,
                points=points,
            ),
            out_shape=kind((tokens, channels), F32),
            in_specs=[vmem] * (len(held[slab_id]) + 3),
            out_specs=vmem,
            scratch_shapes=tables(heads, pltpu.VMEM),
            name=f"solve{slab_id}",
        )(*near(*held[slab_id], side, plan, before))

    ended = solve(1, plan[0:tokens, 0:channels], pltpu.VMEM)
    ended = solve(0, ended, jax.ShapeDtypeStruct)
    return ended[None]


def solution(mesh):
    placed = (
        P(("groups", "seq"), None),
        P("groups", None),
        P("groups"),
        P(),
        P(None, "seq"),
        P(None, "seq"),
        P(None, "seq"),
        P("seq", None),
        P(),
        P(),
        P(),
        P(),
    )
    return jax.shard_map(
        local,
        mesh=mesh,
        in_specs=placed,
        out_specs=P("slab", ("groups", "seq"), None),
        check_vma=False,
    )
```

```python
import functools
import math

import jax
import jax.numpy as jnp
from jax import lax
from jax.experimental import pallas as pl
from jax.experimental.pallas import tpu as pltpu
from jax.sharding import PartitionSpec as P

HEAD_SIZE = 128
F32 = jnp.float32
BF16 = jnp.bfloat16
NT = (((1,), (1,)), ((), ()))
TN = (((0,), (0,)), ((), ()))


def dot(a, b, dims=(((1,), (0,)), ((), ()))):
    return lax.dot_general(a, b, dims, preferred_element_type=F32)


def split2(x):
    high = x.astype(BF16)
    return high, (x - high.astype(F32)).astype(BF16)


def split3(x):
    high = x.astype(BF16)
    mid, low = split2(x - high.astype(F32))
    return high, mid, low


def dot_fine(a, b):
    a_high, a_low = split2(a)
    b_high, b_low = split2(b)
    return dot(
        jnp.concatenate([a_high, a_high, a_low], axis=1),
        jnp.concatenate([b_high, b_low, b_high], axis=1),
        NT,
    )


def dot_short(a, b):
    return dot(a.astype(BF16), b.astype(BF16), NT)


def layout(channels, tokens):
    second = channels
    third = second + channels // 2
    tail = third + channels
    return second, third, tail, tail + 4 + tokens // 2 + tokens


def iotas(rows, columns):
    return (
        lax.broadcasted_iota(jnp.int32, (rows, columns), 0),
        lax.broadcasted_iota(jnp.int32, (rows, columns), 1),
    )


def fold_kernel(
    noise_hbm,
    w_in_hbm,
    wq_hbm,
    wk_hbm,
    wv_hbm,
    wo_hbm,
    wf_hbm,
    scale_hbm,
    shift_hbm,
    out_ref,
    noise,
    w_in,
    w_a,
    w_b,
    w_c,
    wo,
    wf,
    scale,
    shift,
    sems,
    *,
    pieces,
):
    channels, width = w_in.shape
    half = channels // 2
    tokens = noise.shape[0]
    second, third, tail, rows_all = layout(channels, tokens)

    def parts(total):
        last = total[2 * channels : 2 * channels + 8]
        return total[0:channels], total[channels : 2 * channels], last[0:1] + last[1:2]

    used = 0

    def fetch(src, dst):
        nonlocal used
        copy = pltpu.make_async_copy(src, dst, sems.at[used])
        copy.start()
        used += 1
        return copy

    waits = [fetch(w_in_hbm, w_in), fetch(scale_hbm, scale), fetch(shift_hbm, shift)]
    tiles = width // HEAD_SIZE
    cuts = [tiles * k // pieces // 2 * 2 * HEAD_SIZE for k in range(pieces)] + [width]
    pulls = []
    for low, high in zip(cuts, cuts[1:]):
        at = pl.ds(low, high - low)
        pulls.append(
            [
                fetch(src.at[at], dst.at[at])
                for src, dst in ((wq_hbm, w_a), (wk_hbm, w_b), (wv_hbm, w_c))
            ]
        )
    finals = [fetch(wf_hbm, wf), fetch(wo_hbm, wo), fetch(noise_hbm, noise)]
    total = None
    for copy in waits:
        copy.wait()
    factors = scale[...].reshape(1, width)
    shift_high, shift_low = split2(shift[...].reshape(1, width))
    shift_high, shift_low = shift_high.astype(F32), shift_low.astype(F32)
    for low, high, pull in zip(cuts, cuts[1:], pulls):
        for copy in pull:
            copy.wait()
        at = slice(low, high)
        plain = w_in[:, at]
        scaled = plain.astype(F32) * factors[:, at]
        row, _ = iotas(16, high - low)
        vectors = jnp.where(
            row == 0, shift_high[:, at], jnp.where(row == 1, shift_low[:, at], 0.0)
        )
        lift = jnp.concatenate([plain, scaled.astype(BF16), vectors.astype(BF16)], axis=0)
        term = dot(lift, jnp.concatenate([w_a[at], w_b[at], w_c[at]], axis=1))
        total = term if total is None else total + term
    for copy in finals:
        copy.wait()
    out_t = dot(wf[...].astype(BF16), wo[...], NT)
    q0, q1, q2 = parts(total[:, 0:HEAD_SIZE] * (math.log2(math.e) / math.sqrt(HEAD_SIZE)))
    k0, k1, k2 = parts(total[:, HEAD_SIZE : 2 * HEAD_SIZE])
    v0, v1, v2 = parts(total[:, 2 * HEAD_SIZE : 3 * HEAD_SIZE])
    pad = jnp.zeros((7, HEAD_SIZE), F32)
    q_all = jnp.concatenate([q0, q1], axis=0)
    k_all = jnp.concatenate([k0, k1], axis=0)
    form = dot_short(k_all, q_all)
    a_rows = dot_short(jnp.concatenate([k2, pad], axis=0), q_all)
    b_rows = dot_short(jnp.concatenate([q2, pad], axis=0), k_all)
    constant = jnp.sum(k2 * q2)
    p_rows = dot_short(
        jnp.concatenate([v2, pad], axis=0), jnp.concatenate([out_t, out_t], axis=0)
    )
    _, lane = iotas(channels, 2 * channels)
    top, bottom = form[0:channels], form[channels : 2 * channels]
    rolled = pltpu.roll(bottom, channels, 1)
    out_ref[0:channels] = jnp.where(lane < channels, top, top + rolled).astype(BF16)
    out_ref[second:third] = jnp.where(
        lane[0:half] < channels, rolled[0:half], bottom[half:channels]
    ).astype(BF16)
    out_ref[third:tail] = dot_short(out_t, jnp.concatenate([v0, v1], axis=0)).astype(BF16)
    n_high, n_mid, n_low = (part.astype(F32) for part in split3(noise[...]))
    lows = jnp.concatenate([n_low[0 : tokens // 2], n_low[tokens // 2 : tokens]], axis=1)
    row, lane = iotas(4, 2 * channels)
    left = lane < channels
    a_roll = pltpu.roll(a_rows, channels, 1)[0:1]
    b_roll = pltpu.roll(b_rows, channels, 1)[0:1]
    vectors = jnp.where(
        row == 0,
        jnp.where(left, 0.0, a_roll),
        jnp.where(
            row == 1,
            jnp.where(left, a_roll, constant),
            jnp.where(
                row == 2,
                jnp.where(left, 0.0, b_roll),
                jnp.where(left, b_roll, p_rows[0:1]),
            ),
        ),
    )
    out_ref[tail:rows_all] = jnp.concatenate(
        [vectors, lows, jnp.concatenate([n_high, n_mid], axis=1)], axis=0
    ).astype(BF16)


def unpack(pay_ref, base, h, tables, channels, tokens):
    squares, *vectors, start = tables
    second, third, tail, rows_all = layout(channels, tokens)
    folded = pay_ref[pl.ds(base + second, third - second)].astype(F32)
    ext = pay_ref[pl.ds(base + tail, rows_all - tail)].astype(F32)
    at = pl.ds(h * channels, channels)
    squares[at] = jnp.concatenate([folded, pltpu.roll(folded, channels, 1)], axis=0).astype(BF16)
    for i, vector in enumerate(vectors):
        vector[pl.ds(h, 1)] = ext[i : i + 1]
    lows = ext[4 : 4 + tokens // 2]
    pieces = ext[4 + tokens // 2 :]
    low = jnp.concatenate([lows, pltpu.roll(lows, channels, 1)], axis=0)
    start[pl.ds(h * tokens, tokens)] = (pieces + pltpu.roll(pieces, channels, 1)) + low


def side_kernel(
    times_ref,
    counts_ref,
    w_in_ref,
    wf_ref,
    gain_ref,
    out_ref,
    plan_ref,
):
    channels, width = w_in_ref.shape
    w_in = w_in_ref[...]
    gram = dot(w_in, w_in, NT) * (1.0 / width)
    gained = w_in.astype(F32) * gain_ref[...].reshape(1, width)
    skip = dot_fine(wf_ref[...], gained)
    g_high, g_mid, g_low = split3(gram)
    s_high, s_low = split2(skip)
    zero = jnp.zeros_like(s_high)
    out_ref[...] = jnp.concatenate(
        [
            jnp.concatenate([g_high, g_mid], axis=1),
            jnp.concatenate([s_high, s_low], axis=1),
            jnp.concatenate([g_low, zero], axis=1),
            jnp.concatenate([zero, zero], axis=1),
        ],
        axis=0,
    )

    lanes = plan_ref.shape[1]
    points = times_ref.shape[1]

    def level(slab_id, column):
        whole = jnp.zeros((1, lanes), jnp.int32) + times_ref[slab_id, column]
        return whole.astype(F32) / 1000.0

    for k in range(2):
        levels = [level(k, column) for column in range(points)]
        last = jnp.zeros((1, lanes), F32)
        for column in range(points):
            last = jnp.where(column == counts_ref[k], levels[column], last)
        steps = [
            jnp.where(j < counts_ref[k], levels[j + 1] - levels[j], 0.0)
            for j in range(points - 1)
        ]
        rows = levels + steps + [last - levels[0]]
        for i, value in enumerate(rows):
            plan_ref[pl.ds(k * 2 * points + i, 1)] = value


def solve_kernel(
    *refs,
    arrays,
    heads,
    tokens,
    slab_id,
    points,
):
    pays = refs[:arrays]
    side_ref, plan_ref, before_ref, out_ref, *tables = refs[arrays:]
    squares, a_first, a_second, b_first, b_second, start = tables
    slab = lax.axis_index("slab")
    channels = side_ref.shape[1] // 2
    count = heads * tokens
    lanes = count if slab_id == 0 else 2 * count
    second, third, tail, rows_all = layout(channels, tokens)
    fine_most = points - 1

    def block(h):
        at = h * rows_all
        for pay_ref in pays:
            if at < pay_ref.shape[0]:
                return pay_ref, at
            at -= pay_ref.shape[0]

    def rows_of(h, low, high):
        ref, base = block(h)
        return ref[base + low : base + high]

    @pl.when(slab != slab_id)
    def _():
        out_ref[...] = before_ref[...]

    @pl.when(slab == slab_id)
    def _():
        for h in range(heads):
            unpack(*block(h), h, tables, channels, tokens)

        def square(h):
            at = slice(h * channels, (h + 1) * channels)
            return squares[at]

        _, lane = iotas(1, lanes)
        left = lane < count
        constants = jnp.broadcast_to(a_second[:, channels : channels + 1], (heads, lanes))
        vector_maps = jnp.concatenate(
            [
                jnp.concatenate([b_first[...], a_first[...]], axis=0),
                jnp.concatenate([b_second[...], a_second[...]], axis=0),
            ],
            axis=1,
        ).astype(BF16)
        p_row = jnp.sum(b_second[...], axis=0, keepdims=True)
        p_row = jnp.broadcast_to(p_row, (8, 2 * channels))
        p_sum = jnp.broadcast_to(
            jnp.transpose(p_row)[channels : 2 * channels, 0:1], (channels, lanes)
        )
        row, column = iotas(heads, lanes)
        pair_selectors = [
            jnp.where(
                ((row == h) & (column < count)) | ((row == h + 1) & (column >= count)), 1.0, 0.0
            ).astype(BF16)
            for h in range(0, heads, 2)
        ]
        if lanes == count:
            row, _ = iotas(heads, lanes)
            masks = [row == h for h in range(heads)]
        else:
            row, column = iotas(2 * heads, lanes)
            masks = [
                ((row == h) & (column >= count)) | ((row == heads + h) & (column < count))
                for h in range(heads)
            ]
        selectors = [jnp.where(mask, 1.0, 0.0).astype(BF16) for mask in masks]

        def level(k, column):
            row = k * 2 * points + column
            return plan_ref[row : row + 1, 0:lanes]

        def step(k, j):
            return level(k, points + j)

        def span(k):
            return level(k, 2 * points - 1)

        def by_block(row):
            if lanes == count:
                return [row]
            return [jnp.where(left, row, 0.0), jnp.where(left, 0.0, row)]

        def key_side(rows, same):
            turned = jnp.transpose(rows)
            first, last = turned[0:count], turned[count:lanes]
            if same or lanes == count:
                return first[:, 0 : channels + heads].astype(BF16)
            rolled = pltpu.roll(last, channels, 1)
            terms = pltpu.roll(first, channels + heads, 1)
            _, lane = iotas(count, 2 * channels)
            one = jnp.where(lane < channels, first, rolled)
            two = jnp.where(lane < heads, rolled, terms)
            return jnp.concatenate([one, two[:, 0 : 2 * heads]], axis=1).astype(BF16)

        def softmax(scores):
            raised = jnp.exp2(scores - jnp.max(scores, axis=0, keepdims=True))
            return raised, 1.0 / jnp.sum(raised, axis=0, keepdims=True)

        def velocity(u, s, same):
            rounded = u.astype(BF16)
            wide = rounded.astype(F32)
            s2 = s * s
            features = jnp.concatenate(
                [
                    rounded,
                    (s * wide).astype(BF16),
                    (s2 * wide).astype(BF16),
                    jnp.zeros((channels, lanes), BF16),
                ],
                axis=0,
            )
            twice = jnp.concatenate([rounded, rounded], axis=0)
            sides = dot(side_ref[0 : 2 * channels], twice) + dot(
                side_ref[2 * channels : 4 * channels], twice
            )
            norm = jnp.sum(sides[0:channels] * wide, axis=0, keepdims=True)
            r = lax.rsqrt(jnp.maximum(norm, 0.0) + 1e-06)
            maps = [vector_maps]
            for h in range(heads):
                maps.append(jnp.concatenate([rows_of(h, 0, channels), square(h)], axis=1))
            product = dot(jnp.concatenate(maps, axis=0), features)
            values = dot(
                jnp.concatenate(
                    [
                        rows_of(h, third, tail)
                        for h in range(heads)
                    ],
                    axis=0,
                ),
                features[0 : 2 * channels],
            )
            offsets = r * product[heads : 2 * heads] + s2 * constants
            blank = jnp.zeros((channels - heads, lanes), F32)
            keys = key_side(jnp.concatenate([r * wide, r * product[0:heads], blank], axis=0), same)
            at_queries = 2 * heads
            raws = [
                product[at_queries + h * channels : at_queries + (h + 1) * channels]
                for h in range(heads)
            ]
            own_part = r * sides[channels : 2 * channels] + s * p_sum
            if same:
                pairs = []
                for h in range(0, heads, 2):
                    query = (r * jnp.where(left, raws[h], raws[h + 1])).astype(BF16)
                    pairs.append(jnp.concatenate([query, pair_selectors[h // 2]], axis=0))
                joined = dot(keys, jnp.concatenate(pairs, axis=1))
                rhs = []
                for h in range(0, heads, 2):
                    at = h // 2 * lanes
                    offset = jnp.where(left, offsets[h : h + 1], offsets[h + 1 : h + 2])
                    raised, inverse = softmax(joined[:, at : at + lanes] + offset)
                    rhs.append((raised * inverse).astype(BF16))
                values = [
                    r * values[h * channels : (h + 1) * channels] for h in range(heads)
                ]
                lhs = [
                    jnp.concatenate(
                        [
                            jnp.where(left, values[h + k], values[h + k + 2]).astype(BF16)
                            for h in range(0, heads, 4)
                        ],
                        axis=1,
                    )
                    for k in range(2)
                ]
                both = dot(jnp.concatenate(lhs, axis=0), jnp.concatenate(rhs, axis=0))
                mixed = jnp.where(left, both[0:channels], both[channels : 2 * channels])
                return own_part + (mixed + pltpu.roll(mixed, count, 1))
            r_blocks = by_block(r)
            pairs = []
            for h in range(heads):
                query = [(raws[h] * part).astype(BF16) for part in r_blocks]
                pairs.append(jnp.concatenate([*query, selectors[h]], axis=0))
            if lanes == count:
                parts = [dot(keys, pair) for pair in pairs]
            else:
                joined = dot(keys, jnp.concatenate(pairs, axis=1))
                parts = [joined[:, h * lanes : (h + 1) * lanes] for h in range(heads)]
            rhs = []
            for h in range(heads):
                raised, inverse = softmax(parts[h] + offsets[h : h + 1])
                rhs += [(raised * part).astype(BF16) for part in by_block(inverse)]
            values = [
                (r * values[h * channels : (h + 1) * channels]).astype(BF16)
                for h in range(heads)
            ]
            return own_part + dot(
                jnp.concatenate(values, axis=1), jnp.concatenate(rhs, axis=0)
            )

        noise = jnp.transpose(start[...])[0:channels]
        both_slabs = slab_id != 0
        if both_slabs:
            noise = jnp.concatenate([noise, noise], axis=1)
        moved = velocity(noise, level(0, 0), both_slabs)
        first_coarse = noise + span(0) * moved
        if slab_id == 0:
            u = noise + step(0, 0) * moved
            for j in range(1, fine_most):
                u = u + step(0, j) * velocity(u, level(0, j), False)
            ended = first_coarse + (u - first_coarse)
        else:
            u = jnp.where(left, noise + step(0, 0) * moved, first_coarse)
            coarse_old = None
            for j in range(fine_most):
                last = j == fine_most - 1
                s = jnp.where(left, level(1, 0) if last else level(0, j + 1), level(1, j))
                moved = velocity(u, s, False)
                if j == 0:
                    coarse_old = u + span(1) * moved
                u = u + jnp.where(left, span(1) if last else step(0, j + 1), step(1, j)) * moved
            ended = u + pltpu.roll(u - coarse_old, count, 1)
        out_ref[...] = jnp.transpose(ended)[0:tokens, 0:channels]


def exchanged(value, distances):
    groups, size, slabs = (lax.axis_size(axis) for axis in ("groups", "seq", "slab"))
    pairs = []
    for g in range(groups):
        for s in range(size):
            for c in range(slabs):
                to = (g ^ 1, s) if distances[c] is None else (g, s ^ distances[c])
                pairs.append(((g * size + s) * slabs + c, (to[0] * size + to[1]) * slabs + c))
    return lax.ppermute(value, ("groups", "seq", "slab"), pairs)


def local(
    noise,
    timesteps,
    fine_counts,
    w_in,
    w_query,
    w_key,
    w_value,
    w_out,
    w_final,
    mod_scale,
    mod_shift,
    skip_gain,
):
    channels, width = w_in.shape
    tokens = noise.shape[0]
    heads = lax.axis_size("seq")
    count = tokens * heads
    points = timesteps.shape[1]
    *_, rows = layout(channels, tokens)
    wf_t = w_final.T
    vmem = pl.BlockSpec(memory_space=pltpu.VMEM)
    smem = pl.BlockSpec(memory_space=pltpu.SMEM)
    hbm = pl.BlockSpec(memory_space=pl.ANY)

    def near(*values):
        return [pltpu.with_memory_space_constraint(value, pltpu.VMEM) for value in values]

    pieces = 1
    packed = pl.pallas_call(
        functools.partial(fold_kernel, pieces=pieces),
        out_shape=pltpu.VMEM((rows, 2 * channels), BF16),
        in_specs=[hbm] * 9,
        out_specs=vmem,
        scratch_shapes=[
            pltpu.VMEM((tokens, channels), F32),
            pltpu.VMEM((channels, width), BF16),
            pltpu.VMEM((width, HEAD_SIZE), BF16),
            pltpu.VMEM((width, HEAD_SIZE), BF16),
            pltpu.VMEM((width, HEAD_SIZE), BF16),
            pltpu.VMEM((HEAD_SIZE, width), BF16),
            pltpu.VMEM((channels, width), F32),
            pltpu.VMEM((width,), F32),
            pltpu.VMEM((width,), F32),
            pltpu.SemaphoreType.DMA((6 + 3 * pieces,)),
        ],
        name="fold",
    )(noise, w_in, w_query, w_key, w_value, w_out, wf_t, mod_scale, mod_shift)
    swap = [(0, 1), (1, 0)]
    shared = heads == 8 and lax.axis_size("groups") % 2 == 0
    if shared:
        three = [exchanged(packed, pair) for pair in ((3, 6), (2, 5), (1, 7))]
        fourth = exchanged(packed, (None, 4))
        three = jnp.concatenate(three, axis=0)
    else:
        three, stride = packed, heads // 2
        while stride:
            three = jnp.concatenate([three, exchanged(three, (stride, stride))], axis=0)
            stride //= 2

    def tables(n, kind):
        return (
            kind((n * channels, 2 * channels), BF16),
            *(kind((n, 2 * channels), F32) for _ in range(4)),
            kind((n * tokens, 2 * channels), F32),
        )

    side, plan = pl.pallas_call(
        side_kernel,
        out_shape=(
            pltpu.VMEM((4 * channels, 2 * channels), BF16),
            pltpu.VMEM((4 * points, 2 * count), F32),
        ),
        in_specs=[smem, smem, vmem, vmem, vmem],
        out_specs=(vmem,) * 2,
        name="side",
    )(timesteps, fine_counts, w_in, wf_t, skip_gain)
    if shared:
        three, fourth, side, plan = lax.optimization_barrier((three, fourth, side, plan))
        traded = lax.ppermute(three, "slab", swap)
        held = [(packed, three, traded, lax.ppermute(fourth, "slab", swap))]
        held.append((packed, three, traded, fourth))
    else:
        held = [(three,), (three,)]

    def solve(slab_id, before, kind):
        return pl.pallas_call(
            functools.partial(
                solve_kernel,
                arrays=len(held[slab_id]),
                heads=heads,
                tokens=tokens,
                slab_id=slab_id,
                points=points,
            ),
            out_shape=kind((tokens, channels), F32),
            in_specs=[vmem] * (len(held[slab_id]) + 3),
            out_specs=vmem,
            scratch_shapes=tables(heads, pltpu.VMEM),
            name=f"solve{slab_id}",
        )(*near(*held[slab_id], side, plan, before))

    ended = solve(1, plan[0:tokens, 0:channels], pltpu.VMEM)
    ended = solve(0, ended, jax.ShapeDtypeStruct)
    return ended[None]


def solution(mesh):
    placed = (
        P(("groups", "seq"), None),
        P("groups", None),
        P("groups"),
        P(),
        P(None, "seq"),
        P(None, "seq"),
        P(None, "seq"),
        P("seq", None),
        P(),
        P(),
        P(),
        P(),
    )
    return jax.shard_map(
        local,
        mesh=mesh,
        in_specs=placed,
        out_specs=P("slab", ("groups", "seq"), None),
        check_vma=False,
    )
```
